32 devices in a mesh: dp: 4 (over y, core), ctx: 2 (over x), tensor: 4 (over z).
Axes of the slice: x: 2, y: 2, z: 4, core: 2. Of those that a mesh axis runs over, the one named last changes fastest.
Arguments:
- layer_input: bfloat16 [4, 512, 8192], P('dp', ('ctx', 'tensor')), may hold values from -6 to 6
- queries: bfloat16 [4, 512, 8192], P('dp', 'ctx', 'tensor'), may hold values from -12 to 12
- forward_output: bfloat16 [4, 512, 8192], P('dp', 'ctx', 'tensor'), may hold values from -6 to 6
- attention_output_gradient: bfloat16 [4, 512, 8192], P('dp', 'ctx', 'tensor'), may hold values from -6 to 6
- key_weight: bfloat16 [8192, 1024], P(None, 'tensor'), may hold values from -3 to 3
- value_projection_weight: bfloat16 [8192, 1024], P(None, 'tensor'), may hold values from -0.0625 to 0.0625
- segment: int32 [4, 512], P('dp'), may hold values from 0 to 4, as said below
- block_table: int32 [4, 4, 4], P('dp'), may hold values from 0 to 1, as said below
- block_owner: int32 [4, 4], P('dp'), may hold values from 0 to 3, each once within a row
Outputs:
- query_grad: bfloat16 [4, 512, 8192], P('dp', 'ctx', 'tensor')
- input_grad: bfloat16 [4, 512, 8192], P('dp', ('ctx', 'tensor'))
- key_weight_grad: bfloat16 [8192, 1024], P(('dp', 'ctx'), 'tensor')
- value_weight_grad: bfloat16 [8192, 1024], P(('dp', 'ctx'), 'tensor')
The draws below stay inside these ranges and needn't reach their ends.
Inputs may be any that keep to these rules, and one draw needn't show every extreme that they name: Along the logical positions of a group the segment never falls; the prompt (0) comes first and every rollout 1 to 4 is present. block_table[g, b, c] is 1 only where some position of logical block b may read some position of logical block c under the causal and segment rule; block_table[g, b, b] is 1 for every block; other such pairs may be 0. `block_owner`: each group's row holds every logical block once.
All inputs are finite; a program needn't handle non-finite values.
Results may differ from the reference program's by a relative error of at most 0.005.
The reference program's roundings to bfloat16 on the way (of `probs_low` and `score_low`) count: a program that leaves them out, or rounds other values in their place, can miss the bound.
Values may be sent and summed in bfloat16 or wider, within the bound.
A program may use at most 128 MiB of HBM per device.

```python
import math
import jax
import jax.numpy as jnp
from jax import lax

MODEL_WIDTH = 8192
QUERY_HEADS = 64
KEY_VALUE_HEADS = 8
HEAD_SIZE = 128
BLK = 128
NROLL = 4
GROUPS = 4
PACK_TOKENS = 512
NBLK = 4


def truncated_gaussian(key, shape, bound):
    return jnp.clip(jax.random.normal(key, shape, jnp.float32), -bound, bound)


def draw_layer_input(key, part):
    random_seed_key = jax.random.fold_in(key, 11)
    value_tensor = truncated_gaussian(random_seed_key, (GROUPS, PACK_TOKENS, MODEL_WIDTH), 6.0)
    return value_tensor.astype(jnp.bfloat16)


def draw_key_weight(key, part):
    random_seed_key = jax.random.fold_in(key, 21)
    fanin_scale = MODEL_WIDTH ** (-0.5)
    value_tensor = truncated_gaussian(random_seed_key, (MODEL_WIDTH, KEY_VALUE_HEADS * HEAD_SIZE), 6.0) * fanin_scale
    return value_tensor.astype(jnp.bfloat16)


def draw_queries(key, part):
    random_seed_key = jax.random.fold_in(key, 31)
    value_tensor = truncated_gaussian(random_seed_key, (GROUPS, PACK_TOKENS, QUERY_HEADS * HEAD_SIZE), 6.0)
    return value_tensor.astype(jnp.bfloat16)


def tree_layout(key):
    layout_key = jax.random.fold_in(key, 55)
    prompt_jit = max(1, min(BLK // 2, PACK_TOKENS // 32))
    prompt_len = PACK_TOKENS * 5 // 8 + jax.random.randint(jax.random.fold_in(layout_key, 1), (GROUPS, 1), -prompt_jit, prompt_jit + 1)
    remaining = PACK_TOKENS - prompt_len
    roll_jit = max(1, min(BLK // 4, (PACK_TOKENS - PACK_TOKENS * 5 // 8 - prompt_jit) // 16))
    positions = jnp.arange(PACK_TOKENS, dtype=jnp.int32)[None, :]
    segments = jnp.where(positions >= prompt_len, 1, 0).astype(jnp.int32)
    for rollout in range(1, NROLL):
        jitter = jax.random.randint(jax.random.fold_in(layout_key, 10 + rollout), (GROUPS, 1), -roll_jit, roll_jit + 1)
        boundary = prompt_len + remaining * rollout // NROLL + jitter
        segments = segments + jnp.where(positions >= boundary, 1, 0).astype(jnp.int32)
    return segments


def draw_segment(key, part):
    return tree_layout(key)


def draw_block_table(key, part):
    segments = tree_layout(key)
    positions = jnp.arange(PACK_TOKENS, dtype=jnp.int32)
    causal = positions[None, :] <= positions[:, None]
    readable = causal[None] & ((segments[:, None, :] == 0) | (segments[:, None, :] == segments[:, :, None]))
    blocks = readable.reshape(GROUPS, NBLK, BLK, NBLK, BLK).any(axis=(2, 4))
    withheld = jax.random.randint(jax.random.fold_in(key, 77), (GROUPS, NBLK, NBLK), 0, 4) == 0
    diagonal = jnp.arange(NBLK)[:, None] == jnp.arange(NBLK)[None, :]
    blocks = blocks & (jnp.logical_not(withheld) | diagonal[None])
    return jnp.where(blocks, 1, 0).astype(jnp.int32)


def level_of(rng, extent, shards, low, largest):
    level = 1.0
    for position, shards_of in shards:
        heights = jax.random.uniform(jax.random.fold_in(jax.random.fold_in(rng, 6), position), (shards_of,), jnp.float32, low / len(shards), largest / len(shards))
        level = level * jnp.repeat(jnp.exp(heights), extent[position] // shards_of).reshape((-1,) + (1,) * (len(extent) - 1 - position))
    return level


def gaussian(stream_key, extent, scale, most, shards=(), kind=jnp.bfloat16):
    result = jax.random.normal(stream_key, extent, jnp.float32) * scale
    if len(shards) > 0:
        result = level_of(stream_key, extent, shards, -0.22, 0.18) * result
    return jnp.clip(result, min=-most, max=most).astype(kind)


def setup_inputs(seed: int = 0) -> dict:
    seeds = jax.random.split(jax.random.key(seed), 10)
    return {
        "layer_input": draw_layer_input(jax.random.fold_in(seeds[9], 71), 0),
        "queries": draw_queries(jax.random.fold_in(seeds[9], 71), 0),
        "forward_output": gaussian(seeds[2], (GROUPS, PACK_TOKENS, QUERY_HEADS * HEAD_SIZE), 1.0, 6.0, ((0, 4), (1, 2), (2, 4))),
        "attention_output_gradient": gaussian(seeds[3], (GROUPS, PACK_TOKENS, QUERY_HEADS * HEAD_SIZE), 1.0, 6.0, ((0, 4), (1, 2), (2, 4))),
        "key_weight": draw_key_weight(jax.random.fold_in(seeds[9], 71), 0),
        "value_projection_weight": gaussian(seeds[5], (MODEL_WIDTH, KEY_VALUE_HEADS * HEAD_SIZE), MODEL_WIDTH ** -0.5, 0.0625, ((1, 4),)),
        "segment": draw_segment(jax.random.fold_in(seeds[9], 71), 0),
        "block_table": draw_block_table(jax.random.fold_in(seeds[9], 71), 0),
        "block_owner": jax.vmap(lambda own: jax.random.permutation(own, NBLK))(jax.random.split(seeds[8], GROUPS)).reshape((GROUPS, NBLK)).astype(jnp.int32),
    }


def head_grads(scan_entries, allowed):
    query_h, key_h, value_h, saved_h, grad_h = scan_entries
    softmax_scale = 1.0 / math.sqrt(HEAD_SIZE)
    query_f = query_h.astype(jnp.float32)
    key_f = key_h.astype(jnp.float32)
    value_f = value_h.astype(jnp.float32)
    grad_f = grad_h.astype(jnp.float32)
    scores = jnp.einsum('igd,jd->gij', query_f, key_f) * softmax_scale
    scores = jnp.where(allowed[None], scores, -jnp.inf)
    row_max = lax.optimization_barrier(jnp.max(scores, axis=-1, keepdims=True))
    log_norm = row_max + jnp.log(lax.optimization_barrier(jnp.sum(jnp.exp(scores - row_max), axis=-1, keepdims=True)))
    probabilities = jnp.exp(scores - log_norm)
    probs_low = lax.optimization_barrier(probabilities.astype(jnp.bfloat16)).astype(jnp.float32)
    value_gradient_rows = jnp.einsum('gij,igd->jd', probs_low, grad_f)
    prob_grads = jnp.einsum('igd,jd->gij', grad_f, value_f)
    correction = lax.optimization_barrier(jnp.sum(grad_f * saved_h.astype(jnp.float32), axis=-1)).T
    score_low = (probabilities * (prob_grads - correction[:, :, None])).astype(jnp.bfloat16)
    score_low = lax.optimization_barrier(score_low).astype(jnp.float32)
    query_grads = jnp.einsum('gij,jd->igd', score_low, key_f) * softmax_scale
    key_gradient_rows = jnp.einsum('gij,igd->jd', score_low, query_f) * softmax_scale
    return (query_grads, key_gradient_rows, value_gradient_rows)

def reference(layer_input, queries, forward_output, attention_output_gradient, key_weight, value_projection_weight, segment, block_table, block_owner):
    queries_per_group = QUERY_HEADS // KEY_VALUE_HEADS
    query_outs = []
    input_outs = []
    key_weight_total = jnp.zeros((MODEL_WIDTH, KEY_VALUE_HEADS * HEAD_SIZE), jnp.float32)
    value_weight_total = jnp.zeros((MODEL_WIDTH, KEY_VALUE_HEADS * HEAD_SIZE), jnp.float32)
    for head_group in range(GROUPS):
        group_input = layer_input[head_group]
        projected_keys = jnp.dot(group_input, key_weight, preferred_element_type=jnp.float32).astype(jnp.bfloat16)
        projected_values = jnp.dot(group_input, value_projection_weight, preferred_element_type=jnp.float32).astype(jnp.bfloat16)
        row_ids = jnp.arange(PACK_TOKENS, dtype=jnp.int32)
        positions = block_owner[head_group][row_ids // BLK].astype(jnp.int32) * BLK + row_ids % BLK
        segments_at = segment[head_group][positions]
        block_of = positions // BLK
        allowed = positions[None, :] <= positions[:, None]
        allowed = allowed & ((segments_at[None, :] == 0) | (segments_at[None, :] == segments_at[:, None]))
        allowed = allowed & (block_table[head_group][block_of[:, None], block_of[None, :]] == 1)

        def separate_heads(numeric_array):
            return numeric_array.reshape(PACK_TOKENS, KEY_VALUE_HEADS, queries_per_group, HEAD_SIZE).transpose(1, 0, 2, 3)
        scan_entries = (separate_heads(queries[head_group]), projected_keys.reshape(PACK_TOKENS, KEY_VALUE_HEADS, HEAD_SIZE).transpose(1, 0, 2), projected_values.reshape(PACK_TOKENS, KEY_VALUE_HEADS, HEAD_SIZE).transpose(1, 0, 2), separate_heads(forward_output[head_group]), separate_heads(attention_output_gradient[head_group]))
        query_grads, key_gradient_rows, value_gradient_rows = lax.map(lambda entry: head_grads(entry, allowed), scan_entries)
        query_outs.append(query_grads.transpose(1, 0, 2, 3).reshape(PACK_TOKENS, QUERY_HEADS * HEAD_SIZE).astype(jnp.bfloat16))
        key_reduced = key_gradient_rows.transpose(1, 0, 2).reshape(PACK_TOKENS, KEY_VALUE_HEADS * HEAD_SIZE).astype(jnp.bfloat16)
        value_reduced = value_gradient_rows.transpose(1, 0, 2).reshape(PACK_TOKENS, KEY_VALUE_HEADS * HEAD_SIZE).astype(jnp.bfloat16)
        input_sum = jnp.dot(key_reduced, key_weight.T, preferred_element_type=jnp.float32)
        input_sum = input_sum + jnp.dot(value_reduced, value_projection_weight.T, preferred_element_type=jnp.float32)
        input_outs.append(input_sum.astype(jnp.bfloat16))
        key_weight_total = key_weight_total + jnp.dot(group_input.T, key_reduced, preferred_element_type=jnp.float32)
        value_weight_total = value_weight_total + jnp.dot(group_input.T, value_reduced, preferred_element_type=jnp.float32)
    return (jnp.stack(query_outs), jnp.stack(input_outs), key_weight_total.astype(jnp.bfloat16), value_weight_total.astype(jnp.bfloat16))
```

```python
import functools
import math

import jax
import jax.numpy as jnp
from jax import lax
from jax.experimental import pallas as pl
from jax.experimental.pallas import tpu as pltpu
from jax.sharding import PartitionSpec as P

HEAD_SIZE = 128
BLK = 128

MESH = pl.DeviceIdType.MESH
LOW = jnp.bfloat16
FULL = jnp.float32


def grads_kernel(
    nt, nd, nc, heads, groups, subs,
    x_ref, q_ref, o_ref, do_ref, kw_ref, vw_ref, seg_ref, table_ref, owner_ref,
    qg_ref, dx_ref, dkw_ref, dvw_ref,
    g, kwv, wide, xc, q, o, do, kv, bias, corr, acc, part, kz, kp, dx_send,
    x_send, x_recv, w_send, w_recv, p_send, p_recv, f_send, f_recv, s_send, s_recv,
    k_send, k_recv, c_send, c_recv, z_send, z_recv, kp_send, kp_recv, d_send, d_recv,
    local_sem, own_sem, keep_sem,
):
    t = lax.axis_index("tensor")
    d = lax.axis_index("dp")
    c = lax.axis_index("ctx")
    plane = nd * nc
    half = plane // 2
    p = d * nc + c
    h = (d // 2) * nc + c
    core = d % 2
    rows, width = x_ref.shape
    kv2 = kwv.shape[1]
    chunk = width // nt
    piece = chunk // plane
    slice_width = width // plane
    query_rows = nt * rows
    key_rows = nc * query_rows
    sub_rows = rows // subs
    hs = HEAD_SIZE
    pair = 2 * hs
    half_rows = rows // 2
    scale = 1.0 / math.sqrt(hs)

    def at(i, size):
        return pl.ds(pl.multiple_of(i * size, size), size)

    def is_end(b):
        return (b == 0) | (b == nt - 1)

    def x_rows(b):
        return g.at[at(b, rows), :]

    def x_copy(way, s, k, first):
        step = 1 if way == 0 else -1
        b = t - step * (s - 1)
        target = t + step
        ok = (target >= 0) & (target < nt) & (b >= 0) & (b < nt)
        dst = g.at[pl.ds(pl.multiple_of(b * rows + k * sub_rows, sub_rows), sub_rows), :]
        src = x_ref.at[pl.ds(k * sub_rows, sub_rows), :] if first else dst
        return ok, pltpu.make_async_remote_copy(
            src_ref=src, dst_ref=dst, send_sem=x_send.at[way, s - 1, k],
            recv_sem=x_recv.at[way, s - 1, k], device_id={"tensor": target}, device_id_type=MESH,
        )

    def w_copy(r):
        other = (t + r) % nt
        return pltpu.make_async_remote_copy(
            src_ref=kwv.at[pl.ds(pl.multiple_of(other * chunk + p * piece, piece), piece), :],
            dst_ref=wide.at[t, at(p, piece), :],
            send_sem=w_send.at[r - 1], recv_sem=w_recv.at[r - 1],
            device_id={"tensor": other}, device_id_type=MESH,
        )

    def plane_copy(b, r, source):
        other = (p + r) % plane
        return pltpu.make_async_remote_copy(
            src_ref=source.at[:, at(other, slice_width)], dst_ref=xc.at[p, b],
            send_sem=p_send.at[b, r - 1], recv_sem=p_recv.at[b, r - 1],
            device_id={"dp": other // nc, "ctx": other % nc}, device_id_type=MESH,
        )

    def to_plane(b, source):
        for r in range(1, plane):
            plane_copy(b, r, source).start()

    def keep_copy(b):
        return pltpu.make_async_copy(
            x_rows(b).at[:, at(p, slice_width)], xc.at[p, b], keep_sem.at[b]
        )

    def kv_copy(j, b):
        own = kv.at[pl.ds(pl.multiple_of(c * query_rows + b * rows, rows), rows), :]
        return pltpu.make_async_remote_copy(
            src_ref=own, dst_ref=own, send_sem=k_send.at[j - 1, b], recv_sem=k_recv.at[j - 1, b],
            device_id={"ctx": (c + j) % nc}, device_id_type=MESH,
        )

    def wide_at(r, other):
        return wide.at[(t + nt - r) % nt, at(other, piece), :]

    def fan_copy(r, j):
        hh = (h + j) % half
        return pltpu.make_async_remote_copy(
            src_ref=wide_at(r, p), dst_ref=wide_at(r, p),
            send_sem=f_send.at[r - 1, j - 1], recv_sem=f_recv.at[r - 1, j - 1],
            device_id={"dp": (hh // nc) * 2 + core, "ctx": hh % nc}, device_id_type=MESH,
        )

    def sibling_copy(r, j):
        hh = (h + half - j) % half
        other = ((hh // nc) * 2 + core) * nc + hh % nc
        return pltpu.make_async_remote_copy(
            src_ref=wide_at(r, other), dst_ref=wide_at(r, other),
            send_sem=s_send.at[r - 1, j], recv_sem=s_recv.at[r - 1, j],
            device_id={"dp": d + 1 - 2 * core}, device_id_type=MESH,
        )

    def cols(kh):
        return pl.ds(kh * pair, pair)

    def part_copy(j, kh):
        other = (c + j) % nc
        return pltpu.make_async_remote_copy(
            src_ref=acc.at[at(other, query_rows), cols(kh)], dst_ref=part.at[j - 1, :, cols(kh)],
            send_sem=c_send.at[kh, j - 1], recv_sem=c_recv.at[kh, j - 1],
            device_id={"ctx": other}, device_id_type=MESH,
        )

    def z_copy(way, b, kh, e):
        ref = kz.at[b, e, :, cols(kh)]
        return pltpu.make_async_remote_copy(
            src_ref=ref, dst_ref=ref, send_sem=z_send.at[way, b, kh, e],
            recv_sem=z_recv.at[b, kh, e], device_id={"tensor": t + 1 - 2 * way},
            device_id_type=MESH,
        )

    def kp_copy(r, kh):
        other = (p + r) % plane
        ref = kp.at[at(p, query_rows), cols(kh)]
        return pltpu.make_async_remote_copy(
            src_ref=ref, dst_ref=ref, send_sem=kp_send.at[kh, r - 1],
            recv_sem=kp_recv.at[kh, r - 1], device_id={"dp": other // nc, "ctx": other % nc},
            device_id_type=MESH,
        )

    def dx_copy(r, e):
        other = (t + r) % nt
        return pltpu.make_async_remote_copy(
            src_ref=dx_send.at[e, at(other, half_rows), :],
            dst_ref=dx_ref.at[pl.ds(e * half_rows, half_rows), at(t, chunk)],
            send_sem=d_send.at[e, r - 1], recv_sem=d_recv.at[e, r - 1],
            device_id={"tensor": other}, device_id_type=MESH,
        )

    def dx_keep(e):
        return pltpu.make_async_copy(
            dx_send.at[e, at(t, half_rows), :],
            dx_ref.at[pl.ds(e * half_rows, half_rows), at(t, chunk)], own_sem.at[1 + e],
        )

    loads = [
        pltpu.make_async_copy(x_ref, x_rows(t), local_sem.at[0]),
        pltpu.make_async_copy(q_ref, q, local_sem.at[1]),
        pltpu.make_async_copy(o_ref, o, local_sem.at[2]),
        pltpu.make_async_copy(do_ref, do, local_sem.at[3]),
    ]
    weight_loads = []
    for kh in range(heads):
        for which, ref in enumerate((kw_ref, vw_ref)):
            weight_loads.append(pltpu.make_async_copy(
                ref.at[:, pl.ds(kh * hs, hs)], kwv.at[:, pl.ds(kh * pair + which * hs, hs)],
                local_sem.at[4 + 2 * kh + which],
            ))
    for copy in loads + weight_loads:
        copy.start()
    barrier = pltpu.get_barrier_semaphore()
    for r in range(1, nt):
        pl.semaphore_signal(
            barrier, inc=1, device_id={"tensor": (t + r) % nt}, device_id_type=MESH
        )
    for r in range(1, plane):
        other = (p + r) % plane
        pl.semaphore_signal(
            barrier, inc=1, device_id={"dp": other // nc, "ctx": other % nc}, device_id_type=MESH
        )
    pl.semaphore_wait(barrier, nt - 1 + plane - 1)

    for k in range(subs):
        for way in (0, 1):
            ok, copy = x_copy(way, 1, k, True)

            @pl.when(ok)
            def _():
                copy.start()

    to_plane(t, x_ref)
    for copy in loads + weight_loads:
        copy.wait()
    keep_copy(t).start()
    own_wide = pltpu.make_async_copy(kwv.at[at(t, chunk), :], wide.at[t], own_sem.at[0])
    own_wide.start()
    for r in range(1, nt):
        @pl.when(jnp.logical_not(is_end((t + r) % nt)))
        def _():
            w_copy(r).start()

    def iota(axis):
        return lax.broadcasted_iota(jnp.int32, (BLK, BLK), axis)

    blocks = key_rows // BLK
    blocks_here = query_rows // BLK

    @pl.loop(0, blocks)
    def _(kb):
        key_owner = owner_ref[0, kb]
        key_seg = jnp.sum(
            jnp.where(iota(0) == iota(1), seg_ref[pl.ds(key_owner, 1), :], 0), axis=1,
            keepdims=True,
        )
        for qb in range(blocks_here):
            query_owner = owner_ref[0, c * blocks_here + qb]
            query_seg = seg_ref[pl.ds(query_owner, 1), :]
            withheld = 1 - table_ref[query_owner, key_owner]
            key_pos = iota(0) + (key_owner * BLK + withheld * (1 << 20))
            query_pos = iota(1) + query_owner * BLK
            same = (key_seg == 0) | (key_seg == query_seg)
            bias[at(kb, BLK), pl.ds(qb * BLK, BLK)] = jnp.where(
                (key_pos <= query_pos) & same, 0.0, -jnp.inf
            )

    @pl.loop(0, heads * groups)
    def _(i):
        head = at(i, hs)
        product = do[:, head].astype(FULL) * o[:, head].astype(FULL)
        corr[pl.ds(i, 1), :] = jnp.sum(product.T, axis=0, keepdims=True)

    depth = min(1024, width)

    def project(b):
        def step(i, total):
            return total + jnp.dot(
                g[at(b, rows), at(i, depth)], kwv[at(i, depth), :], preferred_element_type=FULL
            )

        total = lax.fori_loop(0, width // depth, step, jnp.zeros((rows, kv2), FULL))
        kv[pl.ds(pl.multiple_of(c * query_rows + b * rows, rows), rows), :] = total.astype(LOW)
        for j in range(1, nc):
            kv_copy(j, b).start()

    project(t)
    for s in range(1, nt):
        for k in range(subs):
            for way in (0, 1):
                b = t - s if way == 0 else t + s

                @pl.when((b >= 0) & (b < nt))
                def _():
                    x_copy(way, s, k, False)[1].wait_recv()

                if s < nt - 1:
                    ok, copy = x_copy(way, s + 1, k, False)

                    @pl.when(ok)
                    def _():
                        copy.start()

        for way in (0, 1):
            b = t - s if way == 0 else t + s

            @pl.when((b >= 0) & (b < nt))
            def _():
                project(b)
                to_plane(b, x_rows(b))
                keep_copy(b).start()

        if s == nt // 2:
            @pl.when(jnp.logical_not(is_end(t)))
            def _():
                for r in range(1, nt):
                    w_copy(r).wait_recv()
                    for j in range(1, half):
                        fan_copy(r, j).start()
                    sibling_copy(r, 0).start()

    for r in range(1, nt):
        @pl.when(is_end((t + r) % nt) & is_end(t))
        def _():
            w_copy(r).start()

    for j in range(1, nc):
        for b in range(nt):
            kv_copy(j, b).wait_recv()

    acc[...] = jnp.zeros_like(acc)
    for kh in range(heads):
        key_cols = pl.ds(kh * pair, hs)
        value_cols = pl.ds(kh * pair + hs, hs)

        @pl.loop(0, groups)
        def _(i):
            head = pl.ds(pl.multiple_of((kh * groups + i) * hs, hs), hs)
            keys = kv[:, key_cols]
            queries = q[:, head]
            grads = do[:, head]
            scores = lax.dot_general(
                keys, queries, (((1,), (1,)), ((), ())), preferred_element_type=FULL
            )
            scores = scores * (scale * math.log2(math.e)) + bias[...]
            top = jnp.max(scores, axis=0, keepdims=True)
            weights = jnp.exp2(scores - top)
            probs = weights * (1.0 / jnp.sum(weights, axis=0, keepdims=True))
            acc[:, value_cols] += jnp.dot(
                probs.astype(LOW), grads, preferred_element_type=FULL
            )
            prob_grads = lax.dot_general(
                kv[:, value_cols], grads, (((1,), (1,)), ((), ())), preferred_element_type=FULL
            )
            score_grads = (
                probs * (prob_grads - corr[pl.ds(kh * groups + i, 1), :])
            ).astype(LOW)
            acc[:, key_cols] += jnp.dot(score_grads, queries, preferred_element_type=FULL)
            query_grads = lax.dot_general(
                score_grads, keys, (((0,), (0,)), ((), ())), preferred_element_type=FULL
            )
            qg_ref[:, head] = (query_grads * scale).astype(LOW)

        acc[:, key_cols] = acc[:, key_cols] * scale
        for j in range(1, nc):
            part_copy(j, kh).start()

    for kh in range(heads):
        for j in range(1, nc):
            part_copy(j, kh).wait_recv()
        total = acc[at(c, query_rows), cols(kh)]
        for j in range(1, nc):
            total = total + part[j - 1, :, cols(kh)]
        total = total.astype(LOW)
        kp[at(p, query_rows), cols(kh)] = total
        by_half = total.reshape(nt, 2, half_rows, pair)
        for e in range(2):
            kz[t, e, :, cols(kh)] = by_half[:, e].reshape(nt * half_rows, pair)
            for way in (0, 1):
                @pl.when(t < nt - 1 if way == 0 else t > 0)
                def _():
                    z_copy(way, t, kh, e).start()

        for r in range(1, plane):
            kp_copy(r, kh).start()

    for r in range(1, nt):
        @pl.when(is_end((t + r) % nt) & jnp.logical_not(is_end(t)))
        def _():
            w_copy(r).start()

    @pl.when(is_end(t))
    def _():
        for r in range(1, nt):
            w_copy(r).wait_recv()
            for j in range(1, half):
                fan_copy(r, j).start()
            sibling_copy(r, 0).start()

    order = sorted(range(nt), key=lambda b: abs(2 * b - nt + 1))

    def relay(b, kh, e):
        @pl.when(b != t)
        def _():
            z_copy(0, b, kh, e).wait_recv()

        @pl.when((b < t) & (t < nt - 1))
        def _():
            z_copy(0, b, kh, e).start()

        @pl.when((b > t) & (t > 0))
        def _():
            z_copy(1, b, kh, e).start()

    for b in order[:-2]:
        for kh in range(heads):
            for e in range(2):
                relay(b, kh, e)
    for r in range(1, nt):
        for j in range(1, half):
            fan_copy(r, j).wait_recv()
            sibling_copy(r, j).start()
    own_wide.wait()
    for r in range(1, nt):
        for j in range(half):
            sibling_copy(r, j).wait_recv()
    tile = min(256, chunk)
    for e in range(2):
        for kh in range(heads):
            for b in order[-2:]:
                relay(b, kh, e)

        @pl.loop(0, chunk // tile)
        def _(n):
            columns = at(n, tile)
            out = None
            for b in range(nt):
                term = lax.dot_general(
                    kz[b, e], wide[b, columns, :], (((1,), (1,)), ((), ())),
                    preferred_element_type=FULL,
                )
                out = term if out is None else out + term
            dx_send[e, :, columns] = out.astype(LOW)

        for r in range(1, nt):
            dx_copy(r, e).start()
        dx_keep(e).start()

    for b in range(nt):
        for r in range(1, plane):
            plane_copy(b, r, x_ref).wait_recv()
        keep_copy(b).wait()
    for kh in range(heads):
        for r in range(1, plane):
            kp_copy(r, kh).wait_recv()
    step_width = min(256, slice_width)
    plane_rows = xc.reshape(plane * nt * rows, slice_width)

    @pl.loop(0, slice_width // step_width)
    def _(m):
        columns = at(m, step_width)
        out = lax.dot_general(
            plane_rows[:, columns], kp[...], (((0,), (0,)), ((), ())),
            preferred_element_type=FULL,
        ).astype(LOW)
        for kh in range(heads):
            dkw_ref[columns, pl.ds(kh * hs, hs)] = out[:, kh * pair:kh * pair + hs]
            dvw_ref[columns, pl.ds(kh * hs, hs)] = out[:, kh * pair + hs:(kh + 1) * pair]

    for s in range(1, nt):
        for k in range(subs):
            for way in (0, 1):
                ok, copy = x_copy(way, s, k, s == 1)

                @pl.when(ok)
                def _():
                    copy.wait_send()

        w_copy(s).wait_send()
        for j in range(1, half):
            fan_copy(s, j).wait_send()
        for j in range(half):
            sibling_copy(s, j).wait_send()
    for b in range(nt):
        for r in range(1, plane):
            plane_copy(b, r, x_ref).wait_send()
        for j in range(1, nc):
            kv_copy(j, b).wait_send()
    for kh in range(heads):
        for j in range(1, nc):
            part_copy(j, kh).wait_send()
        for r in range(1, plane):
            kp_copy(r, kh).wait_send()
        for e in range(2):
            for b in range(nt):
                @pl.when((b <= t) & (t < nt - 1))
                def _():
                    z_copy(0, b, kh, e).wait_send()

                @pl.when((b >= t) & (t > 0))
                def _():
                    z_copy(1, b, kh, e).wait_send()

    for e in range(2):
        for r in range(1, nt):
            dx_copy(r, e).wait()
        dx_keep(e).wait()


def per_device(
    layer_input,
    queries,
    forward_output,
    attention_output_gradient,
    key_weight,
    value_projection_weight,
    segment,
    block_table,
    block_owner,
):
    nt, nd, nc = lax.axis_size("tensor"), lax.axis_size("dp"), lax.axis_size("ctx")
    plane = nd * nc
    half = plane // 2
    rows, width = layer_input.shape[1:]
    query_rows, query_width = queries.shape[1:]
    kv = key_weight.shape[1]
    heads = kv // HEAD_SIZE
    groups = query_width // kv
    blocks = block_owner.shape[1]
    key_rows = nc * query_rows
    chunk = width // nt
    slice_width = width // plane
    subs = min(4, rows // 16)
    dma = pltpu.SemaphoreType.DMA
    hbm = pl.BlockSpec(memory_space=pltpu.HBM)
    vmem = pl.BlockSpec(memory_space=pltpu.VMEM)
    smem = pl.BlockSpec(memory_space=pltpu.SMEM)
    query_grad, input_grad, key_weight_grad, value_weight_grad = pl.pallas_call(
        functools.partial(grads_kernel, nt, nd, nc, heads, groups, subs),
        out_shape=(
            jax.ShapeDtypeStruct((query_rows, query_width), LOW),
            jax.ShapeDtypeStruct((rows, width), LOW),
            jax.ShapeDtypeStruct((slice_width, kv), LOW),
            jax.ShapeDtypeStruct((slice_width, kv), LOW),
        ),
        in_specs=[hbm] * 6 + [vmem, smem, smem],
        out_specs=[vmem] * 4,
        scratch_shapes=[
            pltpu.VMEM((nt * rows, width), LOW),
            pltpu.VMEM((width, 2 * kv), LOW),
            pltpu.VMEM((nt, chunk, 2 * kv), LOW),
            pltpu.VMEM((plane, nt, rows, slice_width), LOW),
            pltpu.VMEM((query_rows, query_width), LOW),
            pltpu.VMEM((query_rows, query_width), LOW),
            pltpu.VMEM((query_rows, query_width), LOW),
            pltpu.VMEM((key_rows, 2 * kv), LOW),
            pltpu.VMEM((key_rows, query_rows), FULL),
            pltpu.VMEM((heads * groups, query_rows), FULL),
            pltpu.VMEM((key_rows, 2 * kv), FULL),
            pltpu.VMEM((nc - 1, query_rows, 2 * kv), FULL),
            pltpu.VMEM((nt, 2, query_rows // 2, 2 * kv), LOW),
            pltpu.VMEM((plane * query_rows, 2 * kv), LOW),
            pltpu.VMEM((2, query_rows // 2, chunk), LOW),
            dma((2, nt - 1, subs)), dma((2, nt - 1, subs)),
            dma((nt - 1,)), dma((nt - 1,)),
            dma((nt, plane - 1)), dma((nt, plane - 1)),
            dma((nt - 1, half - 1)), dma((nt - 1, half - 1)),
            dma((nt - 1, half)), dma((nt - 1, half)),
            dma((nc - 1, nt)), dma((nc - 1, nt)),
            dma((heads, nc - 1)), dma((heads, nc - 1)),
            dma((2, nt, heads, 2)), dma((nt, heads, 2)),
            dma((heads, plane - 1)), dma((heads, plane - 1)),
            dma((2, nt - 1)), dma((2, nt - 1)),
            dma((4 + 2 * heads,)), dma((3,)), dma((nt,)),
        ],
        compiler_params=pltpu.CompilerParams(
            collective_id=0, has_side_effects=True, vmem_limit_bytes=60 << 20
        ),
    )(
        layer_input[0], queries[0], forward_output[0], attention_output_gradient[0],
        key_weight, value_projection_weight,
        segment.reshape(blocks, BLK), block_table[0], block_owner,
    )
    return (query_grad[None], input_grad[None], key_weight_grad, value_weight_grad)


def solution(mesh):
    in_specs = (
        P("dp", ("ctx", "tensor"), None),
        P("dp", "ctx", "tensor"),
        P("dp", "ctx", "tensor"),
        P("dp", "ctx", "tensor"),
        P(None, "tensor"),
        P(None, "tensor"),
        P("dp", None),
        P("dp", None, None),
        P("dp", None),
    )
    out_specs = (
        P("dp", "ctx", "tensor"),
        P("dp", ("ctx", "tensor"), None),
        P(("dp", "ctx"), "tensor"),
        P(("dp", "ctx"), "tensor"),
    )
    return jax.shard_map(
        per_device, mesh=mesh, in_specs=in_specs, out_specs=out_specs, check_vma=False
    )
```

```python
import functools
import math

import jax
import jax.numpy as jnp
from jax import lax
from jax.experimental import pallas as pl
from jax.experimental.pallas import tpu as pltpu
from jax.sharding import PartitionSpec as P

HEAD_SIZE = 128
BLK = 128
UNITS = (3, 5)

MESH = pl.DeviceIdType.MESH
LOW = jnp.bfloat16
FULL = jnp.float32


def grads_kernel(
    nt, nd, nc, heads, groups, subs, end_units, mid_units,
    x_ref, q_ref, o_ref, do_ref, kw_ref, vw_ref, seg_ref, table_ref, owner_ref,
    qg_ref, dx_ref, dkw_ref, dvw_ref,
    g, kwv, wide, xc, q, o, do, kv, bias, corr, acc, part, kz, kp, dx_sum, dx_send,
    x_send, x_recv, w_send, w_recv, p_send, p_recv, f_send, f_recv, s_send, s_recv,
    m_send, m_recv, n_send, n_recv, k_send, k_recv, c_send, c_recv, z_send, z_recv, d_send, d_recv,
    local_sem, own_sem, keep_sem,
):
    t = lax.axis_index("tensor")
    d = lax.axis_index("dp")
    c = lax.axis_index("ctx")
    plane = nd * nc
    half = plane // 2
    p = d * nc + c
    h = (d // 2) * nc + c
    core = d % 2
    rows, width = x_ref.shape
    kv2 = kwv.shape[1]
    unit = wide.shape[2]
    slots = wide.shape[0]
    piece = unit // plane
    slice_width = width // plane
    query_rows = nt * rows
    key_rows = nc * query_rows
    sub_rows = rows // subs
    hs = HEAD_SIZE
    pair = 2 * hs
    half_rows = rows // 2
    scale = 1.0 / math.sqrt(hs)

    def at(i, size):
        return pl.ds(pl.multiple_of(i * size, size), size)

    def is_end(b):
        return (b == 0) | (b == nt - 1)

    def count(b):
        return jnp.where(is_end(b), end_units, mid_units)

    def first(b):
        return jnp.where(b == 0, 0, end_units + (b - 1) * mid_units)

    def beside_end(b):
        return is_end(b) & jnp.logical_not(is_end(t)) & ((b == t + 1) | (b == t - 1))

    far = jnp.where(t < nt // 2, nt - 1, 0)
    ring = nc == 2 and half == 4

    def x_rows(b):
        return g.at[at(b, rows), :]

    def x_copy(way, s, k, first):
        step = 1 if way == 0 else -1
        b = t - step * (s - 1)
        target = t + step
        ok = (target >= 0) & (target < nt) & (b >= 0) & (b < nt)
        dst = g.at[pl.ds(pl.multiple_of(b * rows + k * sub_rows, sub_rows), sub_rows), :]
        src = x_ref.at[pl.ds(k * sub_rows, sub_rows), :] if first else dst
        return ok, pltpu.make_async_remote_copy(
            src_ref=src, dst_ref=dst, send_sem=x_send.at[way, s - 1, k],
            recv_sem=x_recv.at[way, s - 1, k], device_id={"tensor": target}, device_id_type=MESH,
        )

    def w_copy(to, slot):
        begin = (first(to) + slot) * unit + p * piece
        return pltpu.make_async_remote_copy(
            src_ref=kwv.at[pl.ds(pl.multiple_of(begin, piece), piece), :],
            dst_ref=wide.at[slot, t, at(p, piece), :],
            send_sem=w_send.at[to, slot], recv_sem=w_recv.at[t, slot],
            device_id={"tensor": to}, device_id_type=MESH,
        )

    def w_arrival(b, slot):
        ref = wide.at[slot, b, at(p, piece), :]
        return pltpu.make_async_remote_copy(
            src_ref=ref, dst_ref=ref, send_sem=w_send.at[b, slot], recv_sem=w_recv.at[b, slot],
            device_id={"tensor": b}, device_id_type=MESH,
        )

    def send_weights(condition):
        for to in range(nt):
            for slot in range(end_units if to in (0, nt - 1) else mid_units):
                @pl.when((t != to) & condition(to))
                def _():
                    w_copy(to, slot).start()

    def plane_copy(b, r, source):
        other = (p + r) % plane
        return pltpu.make_async_remote_copy(
            src_ref=source.at[:, at(other, slice_width)], dst_ref=xc.at[p, b],
            send_sem=p_send.at[b, r - 1], recv_sem=p_recv.at[b, r - 1],
            device_id={"dp": other // nc, "ctx": other % nc}, device_id_type=MESH,
        )

    def to_plane(b, source):
        for r in range(1, plane):
            plane_copy(b, r, source).start()

    def keep_copy(b):
        return pltpu.make_async_copy(
            x_rows(b).at[:, at(p, slice_width)], xc.at[p, b], keep_sem.at[b]
        )

    def kv_copy(j, b):
        own = kv.at[pl.ds(pl.multiple_of(c * query_rows + b * rows, rows), rows), :]
        return pltpu.make_async_remote_copy(
            src_ref=own, dst_ref=own, send_sem=k_send.at[j - 1, b], recv_sem=k_recv.at[j - 1, b],
            device_id={"ctx": (c + j) % nc}, device_id_type=MESH,
        )

    def same_core(j):
        hh = (h + half - j) % half
        return {"dp": (hh // nc) * 2 + core, "ctx": hh % nc}, (
            ((hh // nc) * 2 + core) * nc + hh % nc
        )

    sibling = {"dp": d + 1 - 2 * core}

    def wide_at(slot, b, other, lo=0, size=None):
        return wide.at[
            slot, b, pl.ds(pl.multiple_of(other * piece + lo, 16), size or piece), :
        ]

    beside_x = d * nc + (c + 1) % nc
    beside_y = ((d + 2) % nd) * nc + c
    across = ((d + 2) % nd) * nc + (c + 1) % nc

    def fan_copy(b, slot, j):
        if ring:
            lower = piece // 2
            ref, to = (
                (wide_at(slot, b, p), {"ctx": (c + 1) % nc}),
                (wide_at(slot, b, p), {"dp": (d + 2) % nd}),
                (wide_at(slot, b, beside_x, 0, lower), {"dp": (d + 2) % nd}),
                (wide_at(slot, b, beside_y, lower, lower), {"ctx": (c + 1) % nc}),
            )[j]
        else:
            ref, to = wide_at(slot, b, p), same_core(half - 1 - j)[0]
        return pltpu.make_async_remote_copy(
            src_ref=ref, dst_ref=ref, send_sem=f_send.at[slot, b, j],
            recv_sem=f_recv.at[slot, b, j], device_id=to, device_id_type=MESH,
        )

    def sibling_copy(b, slot, j):
        if ring:
            other = (p, beside_x, beside_y, across)[j]
        else:
            other = same_core(j)[1]
        ref = wide_at(slot, b, other)
        return pltpu.make_async_remote_copy(
            src_ref=ref, dst_ref=ref, send_sem=s_send.at[slot, b, j],
            recv_sem=s_recv.at[slot, b, j], device_id=sibling, device_id_type=MESH,
        )

    fans = 4 if ring else half - 1

    def each_weight(condition, action):
        for b in range(nt):
            for slot in range(slots):
                @pl.when((b != t) & (slot < count(t)) & condition(b))
                def _():
                    action(b, slot)

    def spread_first(b, slot):
        w_arrival(b, slot).wait_recv()
        for j in range(2 if ring else fans):
            fan_copy(b, slot, j).start()
        sibling_copy(b, slot, 0).start()

    def spread_second(b, slot):
        if ring:
            for j in range(2):
                fan_copy(b, slot, j).wait_recv()
                fan_copy(b, slot, 2 + j).start()
                sibling_copy(b, slot, 1 + j).start()

    def spread_third(b, slot):
        if ring:
            for j in (2, 3):
                fan_copy(b, slot, j).wait_recv()
            sibling_copy(b, slot, 3).start()
        else:
            for j in range(fans):
                fan_copy(b, slot, j).wait_recv()
                sibling_copy(b, slot, j + 1).start()

    def early(b):
        return beside_end(b)

    def late(b):
        return jnp.logical_not(beside_end(b))

    def cols(kh):
        return pl.ds(kh * pair, pair)

    def part_copy(j, kh):
        other = (c + j) % nc
        return pltpu.make_async_remote_copy(
            src_ref=acc.at[at(other, query_rows), cols(kh)], dst_ref=part.at[j - 1, :, cols(kh)],
            send_sem=c_send.at[kh, j - 1], recv_sem=c_recv.at[kh, j - 1],
            device_id={"ctx": other}, device_id_type=MESH,
        )

    def z_copy(way, b, kh, e):
        ref = kz.at[b, e, :, cols(kh)]
        return pltpu.make_async_remote_copy(
            src_ref=ref, dst_ref=ref, send_sem=z_send.at[way, b, kh, e],
            recv_sem=z_recv.at[b, kh, e], device_id={"tensor": t + 1 - 2 * way},
            device_id_type=MESH,
        )

    def kp_at(other, kh):
        return kp.at[at(other, query_rows), cols(kh)]

    def kp_copy(j, kh):
        return pltpu.make_async_remote_copy(
            src_ref=kp_at(p, kh), dst_ref=kp_at(p, kh), send_sem=m_send.at[kh, j],
            recv_sem=m_recv.at[kh, j], device_id=same_core(half - 1 - j)[0],
            device_id_type=MESH,
        )

    def kp_sibling(j, kh):
        ref = kp_at(same_core(j)[1], kh)
        return pltpu.make_async_remote_copy(
            src_ref=ref, dst_ref=ref, send_sem=n_send.at[kh, j], recv_sem=n_recv.at[kh, j],
            device_id=sibling, device_id_type=MESH,
        )

    def dx_columns(b, slot):
        return pl.ds(pl.multiple_of((first(b) + slot) * unit, unit), unit)

    def dx_copy(r, e, slot):
        other = (t + r) % nt
        return pltpu.make_async_remote_copy(
            src_ref=dx_send.at[e, slot, at(other, half_rows), :],
            dst_ref=dx_ref.at[0, pl.ds(e * half_rows, half_rows), dx_columns(t, slot)],
            send_sem=d_send.at[e, slot, r - 1], recv_sem=d_recv.at[e, slot, r - 1],
            device_id={"tensor": other}, device_id_type=MESH,
        )

    def dx_arrival(r, e, slot):
        b = (t + nt - r) % nt
        ref = dx_ref.at[0, pl.ds(e * half_rows, half_rows), dx_columns(b, slot)]
        return pltpu.make_async_remote_copy(
            src_ref=ref, dst_ref=ref, send_sem=d_send.at[e, slot, r - 1],
            recv_sem=d_recv.at[e, slot, r - 1], device_id={"tensor": b}, device_id_type=MESH,
        )

    def dx_keep(e, slot):
        return pltpu.make_async_copy(
            dx_send.at[e, slot, at(t, half_rows), :],
            dx_ref.at[0, pl.ds(e * half_rows, half_rows), dx_columns(t, slot)],
            own_sem.at[1 + e, slot],
        )

    loads = [
        pltpu.make_async_copy(x_ref, x_rows(t), local_sem.at[0]),
        pltpu.make_async_copy(q_ref, q, local_sem.at[1]),
        pltpu.make_async_copy(o_ref, o, local_sem.at[2]),
        pltpu.make_async_copy(do_ref, do, local_sem.at[3]),
    ]
    weight_loads = []
    for kh in range(heads):
        for which, ref in enumerate((kw_ref, vw_ref)):
            weight_loads.append(pltpu.make_async_copy(
                ref.at[:, pl.ds(kh * hs, hs)], kwv.at[:, pl.ds(kh * pair + which * hs, hs)],
                local_sem.at[4 + 2 * kh + which],
            ))
    for copy in loads + weight_loads:
        copy.start()
    barrier = pltpu.get_barrier_semaphore()
    for r in range(1, nt):
        pl.semaphore_signal(
            barrier, inc=1, device_id={"tensor": (t + r) % nt}, device_id_type=MESH
        )
    for r in range(1, plane):
        other = (p + r) % plane
        pl.semaphore_signal(
            barrier, inc=1, device_id={"dp": other // nc, "ctx": other % nc}, device_id_type=MESH
        )
    pl.semaphore_wait(barrier, nt - 1 + plane - 1)

    for k in range(subs):
        for way in (0, 1):
            ok, copy = x_copy(way, 1, k, True)

            @pl.when(ok)
            def _():
                copy.start()

    to_plane(t, x_ref)
    for copy in loads + weight_loads:
        copy.wait()
    keep_copy(t).start()
    def own_wide(slot):
        return pltpu.make_async_copy(
            kwv.at[pl.ds(pl.multiple_of((first(t) + slot) * unit, unit), unit), :],
            wide.at[slot, t], own_sem.at[0, slot],
        )

    def each_own(action):
        for slot in range(slots):
            @pl.when(slot < count(t))
            def _():
                action(slot)

    each_own(lambda slot: own_wide(slot).start())
    send_weights(lambda to: is_end(t) & (not to in (0, nt - 1)) & ((t == to + 1) | (t == to - 1)))

    def iota(axis):
        return lax.broadcasted_iota(jnp.int32, (BLK, BLK), axis)

    blocks = key_rows // BLK
    blocks_here = query_rows // BLK

    @pl.loop(0, blocks)
    def _(kb):
        key_owner = owner_ref[0, kb]
        key_seg = jnp.sum(
            jnp.where(iota(0) == iota(1), seg_ref[pl.ds(key_owner, 1), :], 0), axis=1,
            keepdims=True,
        )
        for qb in range(blocks_here):
            query_owner = owner_ref[0, c * blocks_here + qb]
            query_seg = seg_ref[pl.ds(query_owner, 1), :]
            withheld = 1 - table_ref[query_owner, key_owner]
            key_pos = iota(0) + (key_owner * BLK + withheld * (1 << 20))
            query_pos = iota(1) + query_owner * BLK
            same = (key_seg == 0) | (key_seg == query_seg)
            bias[at(kb, BLK), pl.ds(qb * BLK, BLK)] = jnp.where(
                (key_pos <= query_pos) & same, 0.0, -jnp.inf
            )

    @pl.loop(0, heads * groups)
    def _(i):
        head = at(i, hs)
        product = do[:, head].astype(FULL) * o[:, head].astype(FULL)
        corr[pl.ds(i, 1), :] = jnp.sum(product.T, axis=0, keepdims=True)

    depth = min(1024, width)

    def project(b):
        def step(i, total):
            return total + jnp.dot(
                g[at(b, rows), at(i, depth)], kwv[at(i, depth), :], preferred_element_type=FULL
            )

        total = lax.fori_loop(0, width // depth, step, jnp.zeros((rows, kv2), FULL))
        kv[pl.ds(pl.multiple_of(c * query_rows + b * rows, rows), rows), :] = total.astype(LOW)
        for j in range(1, nc):
            kv_copy(j, b).start()

    project(t)
    for s in range(1, nt):
        for k in range(subs):
            for way in (0, 1):
                b = t - s if way == 0 else t + s

                @pl.when((b >= 0) & (b < nt))
                def _():
                    x_copy(way, s, k, False)[1].wait_recv()

                if s < nt - 1:
                    ok, copy = x_copy(way, s + 1, k, False)

                    @pl.when(ok)
                    def _():
                        copy.start()

        for way in (0, 1):
            b = t - s if way == 0 else t + s

            @pl.when((b >= 0) & (b < nt))
            def _():
                project(b)
                keep_copy(b).start()

            @pl.when((b >= 0) & (b < nt) & (b != far))
            def _():
                to_plane(b, x_rows(b))

        if s == 1:
            send_weights(
                lambda to: jnp.logical_not(is_end(t) & ((t == to + 1) | (t == to - 1)))
                & (not to in (0, nt - 1))
            )
            each_weight(early, spread_first)
        if s == nt // 2:
            each_weight(early, spread_second)

    send_weights(lambda to: is_end(t) & (to in (0, nt - 1)))
    for j in range(1, nc):
        for b in range(nt):
            kv_copy(j, b).wait_recv()

    acc[...] = jnp.zeros_like(acc)
    for kh in range(heads):
        key_cols = pl.ds(kh * pair, hs)
        value_cols = pl.ds(kh * pair + hs, hs)

        @pl.loop(0, groups)
        def _(i):
            head = pl.ds(pl.multiple_of((kh * groups + i) * hs, hs), hs)
            keys = kv[:, key_cols]
            queries = q[:, head]
            grads = do[:, head]
            scores = lax.dot_general(
                keys, queries, (((1,), (1,)), ((), ())), preferred_element_type=FULL
            )
            scores = scores * (scale * math.log2(math.e)) + bias[...]
            top = jnp.max(scores, axis=0, keepdims=True)
            weights = jnp.exp2(scores - top)
            probs = weights * (1.0 / jnp.sum(weights, axis=0, keepdims=True))
            acc[:, value_cols] += jnp.dot(
                probs.astype(LOW), grads, preferred_element_type=FULL
            )
            prob_grads = lax.dot_general(
                kv[:, value_cols], grads, (((1,), (1,)), ((), ())), preferred_element_type=FULL
            )
            score_grads = (
                probs * (prob_grads - corr[pl.ds(kh * groups + i, 1), :])
            ).astype(LOW)
            acc[:, key_cols] += jnp.dot(score_grads, queries, preferred_element_type=FULL)
            query_grads = lax.dot_general(
                score_grads, keys, (((0,), (0,)), ((), ())), preferred_element_type=FULL
            )
            qg_ref[0, :, head] = (query_grads * scale).astype(LOW)

        acc[:, key_cols] = acc[:, key_cols] * scale
        for j in range(1, nc):
            part_copy(j, kh).start()
        if kh == 0:
            each_weight(early, spread_third)
            each_weight(late, spread_first)

    send_weights(lambda to: jnp.logical_not(is_end(t)) & (to in (0, nt - 1)))

    for kh in range(heads):
        for j in range(1, nc):
            part_copy(j, kh).wait_recv()
        total = acc[at(c, query_rows), cols(kh)]
        for j in range(1, nc):
            total = total + part[j - 1, :, cols(kh)]
        total = total.astype(LOW)
        kp[at(p, query_rows), cols(kh)] = total
        by_half = total.reshape(nt, 2, half_rows, pair)
        for e in range(2):
            kz[t, e, :, cols(kh)] = by_half[:, e].reshape(nt * half_rows, pair)
            for way in (0, 1):
                @pl.when(t < nt - 1 if way == 0 else t > 0)
                def _():
                    z_copy(way, t, kh, e).start()

    each_weight(late, spread_second)
    for kh in range(heads):
        for j in range(half - 1):
            kp_copy(j, kh).start()
        kp_sibling(0, kh).start()
    to_plane(far, x_rows(far))

    ends = (0, nt - 1)
    inner = [b for b in range(nt) if b not in ends]
    near = jnp.where(t < nt // 2, 0, nt - 1)
    tile = min(256, unit)

    def relay(b, kh, e):
        @pl.when(b != t)
        def _():
            z_copy(0, b, kh, e).wait_recv()

        @pl.when((b < t) & (t < nt - 1))
        def _():
            z_copy(0, b, kh, e).start()

        @pl.when((b > t) & (t > 0))
        def _():
            z_copy(1, b, kh, e).start()

    def product(left, slot, b, columns):
        return lax.dot_general(
            left, wide[slot, b, columns, :], (((1,), (1,)), ((), ())),
            preferred_element_type=FULL,
        )

    for b in sorted(inner, key=lambda b: abs(2 * b - nt + 1)):
        for kh in range(heads):
            for e in range(2):
                relay(b, kh, e)
    each_weight(late, spread_third)
    each_own(lambda slot: own_wide(slot).wait())

    def spread_done(b, slot):
        for j in range(half):
            sibling_copy(b, slot, j).wait_recv()

    each_weight(lambda b: True, spread_done)

    def input_grads_inner(slot):
        @pl.loop(0, unit // tile)
        def _(n):
            columns = at(n, tile)
            out = None
            for b in inner:
                term = product(kz[b].reshape(query_rows, kv2), slot, b, columns)
                out = term if out is None else out + term
            dx_sum[slot, :, columns] = out

    def input_grads_near(slot):
        @pl.loop(0, unit // tile)
        def _(n):
            columns = at(n, tile)
            dx_sum[slot, :, columns] += product(
                kz[near].reshape(query_rows, kv2), slot, near, columns
            )

    each_own(input_grads_inner)
    for kh in range(heads):
        for e in range(2):
            relay(near, kh, e)
    each_own(input_grads_near)
    for e in range(2):
        for kh in range(heads):
            relay(far, kh, e)

        def input_grads(slot):
            @pl.loop(0, unit // tile)
            def _(n):
                columns = at(n, tile)
                part_rows = pl.ds(e * nt * half_rows, nt * half_rows)
                dx_send[e, slot, :, columns] = (
                    dx_sum[slot, part_rows, columns] + product(kz[far, e], slot, far, columns)
                ).astype(LOW)

            for r in range(1, nt):
                dx_copy(r, e, slot).start()
            dx_keep(e, slot).start()

        each_own(input_grads)

    for b in range(nt):
        for r in range(1, plane):
            plane_copy(b, r, x_ref).wait_recv()
        keep_copy(b).wait()
    for kh in range(heads):
        for j in range(half - 1):
            kp_copy(j, kh).wait_recv()
            kp_sibling(j + 1, kh).start()
    for kh in range(heads):
        for j in range(half):
            kp_sibling(j, kh).wait_recv()
    step_width = min(256, slice_width)
    plane_rows = xc.reshape(plane * nt * rows, slice_width)

    @pl.loop(0, slice_width // step_width)
    def _(m):
        columns = at(m, step_width)
        out = lax.dot_general(
            plane_rows[:, columns], kp[...], (((0,), (0,)), ((), ())),
            preferred_element_type=FULL,
        ).astype(LOW)
        for kh in range(heads):
            dkw_ref[columns, pl.ds(kh * hs, hs)] = out[:, kh * pair:kh * pair + hs]
            dvw_ref[columns, pl.ds(kh * hs, hs)] = out[:, kh * pair + hs:(kh + 1) * pair]

    for s in range(1, nt):
        for k in range(subs):
            for way in (0, 1):
                ok, copy = x_copy(way, s, k, s == 1)

                @pl.when(ok)
                def _():
                    copy.wait_send()

    for to in range(nt):
        for slot in range(end_units if to in (0, nt - 1) else mid_units):
            @pl.when(t != to)
            def _():
                w_copy(to, slot).wait_send()

    def spread_sent(b, slot):
        for j in range(fans):
            fan_copy(b, slot, j).wait_send()
        for j in range(half):
            sibling_copy(b, slot, j).wait_send()

    each_weight(lambda b: True, spread_sent)
    for b in range(nt):
        for r in range(1, plane):
            plane_copy(b, r, x_ref).wait_send()
        for j in range(1, nc):
            kv_copy(j, b).wait_send()
    for kh in range(heads):
        for j in range(1, nc):
            part_copy(j, kh).wait_send()
        for j in range(half - 1):
            kp_copy(j, kh).wait_send()
        for j in range(half):
            kp_sibling(j, kh).wait_send()
        for e in range(2):
            for b in range(nt):
                @pl.when((b <= t) & (t < nt - 1))
                def _():
                    z_copy(0, b, kh, e).wait_send()

                @pl.when((b >= t) & (t > 0))
                def _():
                    z_copy(1, b, kh, e).wait_send()

    for e in range(2):
        def sent(slot):
            for r in range(1, nt):
                dx_copy(r, e, slot).wait_send()
            dx_keep(e, slot).wait()

        each_own(sent)
        for r in range(1, nt):
            for slot in range(slots):
                @pl.when(slot < count((t + nt - r) % nt))
                def _():
                    dx_arrival(r, e, slot).wait_recv()


def per_device(
    layer_input,
    queries,
    forward_output,
    attention_output_gradient,
    key_weight,
    value_projection_weight,
    segment,
    block_table,
    block_owner,
):
    nt, nd, nc = lax.axis_size("tensor"), lax.axis_size("dp"), lax.axis_size("ctx")
    plane = nd * nc
    half = plane // 2
    rows, width = layer_input.shape[1:]
    query_rows, query_width = queries.shape[1:]
    kv = key_weight.shape[1]
    heads = kv // HEAD_SIZE
    groups = query_width // kv
    blocks = block_owner.shape[1]
    key_rows = nc * query_rows
    end_units, mid_units = UNITS if nt == 4 else (1, 1)
    unit = width // (2 * end_units + (nt - 2) * mid_units)
    slots = max(end_units, mid_units)
    fans = 4 if nc == 2 and half == 4 else half - 1
    slice_width = width // plane
    subs = min(4, rows // 16)
    dma = pltpu.SemaphoreType.DMA
    hbm = pl.BlockSpec(memory_space=pltpu.HBM)
    vmem = pl.BlockSpec(memory_space=pltpu.VMEM)
    smem = pl.BlockSpec(memory_space=pltpu.SMEM)
    query_grad, input_grad, key_weight_grad, value_weight_grad = pl.pallas_call(
        functools.partial(grads_kernel, nt, nd, nc, heads, groups, subs, end_units, mid_units),
        out_shape=(
            jax.ShapeDtypeStruct((1, query_rows, query_width), LOW),
            jax.ShapeDtypeStruct((1, rows, width), LOW),
            jax.ShapeDtypeStruct((slice_width, kv), LOW),
            jax.ShapeDtypeStruct((slice_width, kv), LOW),
        ),
        in_specs=[hbm] * 6 + [vmem, smem, smem],
        out_specs=[vmem] * 4,
        scratch_shapes=[
            pltpu.VMEM((nt * rows, width), LOW),
            pltpu.VMEM((width, 2 * kv), LOW),
            pltpu.VMEM((slots, nt, unit, 2 * kv), LOW),
            pltpu.VMEM((plane, nt, rows, slice_width), LOW),
            pltpu.VMEM((query_rows, query_width), LOW),
            pltpu.VMEM((query_rows, query_width), LOW),
            pltpu.VMEM((query_rows, query_width), LOW),
            pltpu.VMEM((key_rows, 2 * kv), LOW),
            pltpu.VMEM((key_rows, query_rows), FULL),
            pltpu.VMEM((heads * groups, query_rows), FULL),
            pltpu.VMEM((key_rows, 2 * kv), FULL),
            pltpu.VMEM((nc - 1, query_rows, 2 * kv), FULL),
            pltpu.VMEM((nt, 2, query_rows // 2, 2 * kv), LOW),
            pltpu.VMEM((plane * query_rows, 2 * kv), LOW),
            pltpu.VMEM((slots, query_rows, unit), FULL),
            pltpu.VMEM((2, slots, query_rows // 2, unit), LOW),
            dma((2, nt - 1, subs)), dma((2, nt - 1, subs)),
            dma((nt, slots)), dma((nt, slots)),
            dma((nt, plane - 1)), dma((nt, plane - 1)),
            dma((slots, nt, fans)), dma((slots, nt, fans)),
            dma((slots, nt, half)), dma((slots, nt, half)),
            dma((heads, half - 1)), dma((heads, half - 1)),
            dma((heads, half)), dma((heads, half)),
            dma((nc - 1, nt)), dma((nc - 1, nt)),
            dma((heads, nc - 1)), dma((heads, nc - 1)),
            dma((2, nt, heads, 2)), dma((nt, heads, 2)),
            dma((2, slots, nt - 1)), dma((2, slots, nt - 1)),
            dma((4 + 2 * heads,)), dma((3, slots)), dma((nt,)),
        ],
        compiler_params=pltpu.CompilerParams(
            collective_id=0, has_side_effects=True, vmem_limit_bytes=60 << 20
        ),
    )(
        layer_input[0], queries[0], forward_output[0], attention_output_gradient[0],
        key_weight, value_projection_weight,
        segment.reshape(blocks, BLK), block_table[0], block_owner,
    )
    return (query_grad, input_grad, key_weight_grad, value_weight_grad)


def solution(mesh):
    in_specs = (
        P("dp", ("ctx", "tensor"), None),
        P("dp", "ctx", "tensor"),
        P("dp", "ctx", "tensor"),
        P("dp", "ctx", "tensor"),
        P(None, "tensor"),
        P(None, "tensor"),
        P("dp", None),
        P("dp", None, None),
        P("dp", None),
    )
    out_specs = (
        P("dp", "ctx", "tensor"),
        P("dp", ("ctx", "tensor"), None),
        P(("dp", "ctx"), "tensor"),
        P(("dp", "ctx"), "tensor"),
    )
    return jax.shard_map(
        per_device, mesh=mesh, in_specs=in_specs, out_specs=out_specs, check_vma=False
    )
```

```python
import functools
import math

import jax
import jax.numpy as jnp
from jax import lax
from jax.experimental import pallas as pl
from jax.experimental.pallas import tpu as pltpu
from jax.sharding import PartitionSpec as P

HEAD_SIZE = 128
BLK = 128
UNITS = (0, 4)

MESH = pl.DeviceIdType.MESH
LOW = jnp.bfloat16
FULL = jnp.float32


def grads_kernel(
    nt, nd, nc, heads, groups, subs, end_units, mid_units,
    x_ref, q_ref, o_ref, do_ref, kw_ref, vw_ref, seg_ref, table_ref, owner_ref,
    qg_ref, dx_ref, dkw_ref, dvw_ref,
    g, kwv, wide, xc, q, o, do, kv, bias, corr, acc, part, kz, kp, dx_sum, dx_send,
    x_send, x_recv, w_send, w_recv, p_send, p_recv, f_send, f_recv, s_send, s_recv,
    m_send, m_recv, n_send, n_recv, k_send, k_recv, c_send, c_recv, z_send, z_recv, d_send, d_recv,
    local_sem, own_sem, keep_sem,
):
    t = lax.axis_index("tensor")
    d = lax.axis_index("dp")
    c = lax.axis_index("ctx")
    plane = nd * nc
    half = plane // 2
    p = d * nc + c
    h = (d // 2) * nc + c
    core = d % 2
    rows, width = x_ref.shape
    kv2 = kwv.shape[1]
    unit = wide.shape[2]
    slots = wide.shape[0]
    piece = unit // plane
    slice_width = width // plane
    query_rows = nt * rows
    key_rows = nc * query_rows
    sub_rows = rows // subs
    hs = HEAD_SIZE
    pair = 2 * hs
    half_rows = rows // 2
    scale = 1.0 / math.sqrt(hs)

    def at(i, size):
        return pl.ds(pl.multiple_of(i * size, size), size)

    def is_end(b):
        return (b == 0) | (b == nt - 1)

    def count(b):
        return jnp.where(is_end(b), end_units, mid_units)

    def first(b):
        return jnp.where(b == 0, 0, end_units + (b - 1) * mid_units)

    def beside_end(b):
        return ring & is_end(b) & ((b == t + 1) | (b == t - 1))

    def takes_part(b):
        return (b >= 0) & (b < nt) & (count(b) > 0)

    far = jnp.where(t < nt // 2, nt - 1, 0)
    ring = nt == 4 and nc == 2 and half == 4 and end_units == 0

    def x_rows(b):
        return g.at[at(b, rows), :]

    def x_copy(way, s, k, first):
        step = 1 if way == 0 else -1
        b = t - step * (s - 1)
        target = t + step
        ok = (target >= 0) & (target < nt) & (b >= 0) & (b < nt)
        dst = g.at[pl.ds(pl.multiple_of(b * rows + k * sub_rows, sub_rows), sub_rows), :]
        src = x_ref.at[pl.ds(k * sub_rows, sub_rows), :] if first else dst
        return ok, pltpu.make_async_remote_copy(
            src_ref=src, dst_ref=dst, send_sem=x_send.at[way, s - 1, k],
            recv_sem=x_recv.at[way, s - 1, k], device_id={"tensor": target}, device_id_type=MESH,
        )

    def w_copy(to, slot, direct):
        share, size = (core, unit // 2) if direct else (p, piece)
        begin = (first(to) + slot) * unit + share * size
        return pltpu.make_async_remote_copy(
            src_ref=kwv.at[pl.ds(pl.multiple_of(begin, size), size), :],
            dst_ref=wide.at[slot, t, at(share, size), :],
            send_sem=w_send.at[to, slot], recv_sem=w_recv.at[t, slot],
            device_id={"tensor": to}, device_id_type=MESH,
        )

    def w_half(b, slot):
        return wide.at[slot, b, at(core, unit // 2), :]

    def w_arrival(b, slot, direct):
        ref = w_half(b, slot) if direct else wide.at[slot, b, at(p, piece), :]
        return pltpu.make_async_remote_copy(
            src_ref=ref, dst_ref=ref, send_sem=w_send.at[b, slot], recv_sem=w_recv.at[b, slot],
            device_id={"tensor": b}, device_id_type=MESH,
        )

    def each_target(direct, action):
        for slot in range(slots):
            for to in range(nt):
                if slot < (end_units if to in (0, nt - 1) else mid_units):
                    beside = is_end(t) & ((t == to + 1) | (t == to - 1)) & ring
                    good = beside if direct else (t != to) & jnp.logical_not(beside)

                    @pl.when(good)
                    def _():
                        action(w_copy(to, slot, direct), to)

    def send_weights(direct, condition):
        def send(copy, to):
            @pl.when(condition(to))
            def _():
                copy.start()

        each_target(direct, send)

    def plane_copy(b, r, source):
        other = (p + r) % plane
        return pltpu.make_async_remote_copy(
            src_ref=source.at[:, at(other, slice_width)], dst_ref=xc.at[p, b],
            send_sem=p_send.at[b, r - 1], recv_sem=p_recv.at[b, r - 1],
            device_id={"dp": other // nc, "ctx": other % nc}, device_id_type=MESH,
        )

    def to_plane(b, source):
        for r in range(1, plane):
            plane_copy(b, r, source).start()

    def keep_copy(b):
        return pltpu.make_async_copy(
            x_rows(b).at[:, at(p, slice_width)], xc.at[p, b], keep_sem.at[b]
        )

    def kv_copy(j, b):
        own = kv.at[pl.ds(pl.multiple_of(c * query_rows + b * rows, rows), rows), :]
        return pltpu.make_async_remote_copy(
            src_ref=own, dst_ref=own, send_sem=k_send.at[j - 1, b], recv_sem=k_recv.at[j - 1, b],
            device_id={"ctx": (c + j) % nc}, device_id_type=MESH,
        )

    def same_core(j):
        hh = (h + half - j) % half
        return {"dp": (hh // nc) * 2 + core, "ctx": hh % nc}, (
            ((hh // nc) * 2 + core) * nc + hh % nc
        )

    sibling = {"dp": d + 1 - 2 * core}

    def wide_at(slot, b, other, lo=0, size=None):
        return wide.at[
            slot, b, pl.ds(pl.multiple_of(other * piece + lo, 16), size or piece), :
        ]

    beside_x = d * nc + (c + 1) % nc
    beside_y = ((d + 2) % nd) * nc + c
    across = ((d + 2) % nd) * nc + (c + 1) % nc

    def fan_copy(b, slot, j):
        if ring:
            lower = piece // 2
            ref, to = (
                (wide_at(slot, b, p), {"ctx": (c + 1) % nc}),
                (wide_at(slot, b, p), {"dp": (d + 2) % nd}),
                (wide_at(slot, b, beside_x, 0, lower), {"dp": (d + 2) % nd}),
                (wide_at(slot, b, beside_y, lower, lower), {"ctx": (c + 1) % nc}),
            )[j]
        else:
            ref, to = wide_at(slot, b, p), same_core(half - 1 - j)[0]
        return pltpu.make_async_remote_copy(
            src_ref=ref, dst_ref=ref, send_sem=f_send.at[slot, b, j],
            recv_sem=f_recv.at[slot, b, j], device_id=to, device_id_type=MESH,
        )

    def sibling_copy(b, slot, j):
        if ring:
            other = (p, beside_x, beside_y, across)[j]
        else:
            other = same_core(j)[1]
        ref = wide_at(slot, b, other)
        return pltpu.make_async_remote_copy(
            src_ref=ref, dst_ref=ref, send_sem=s_send.at[slot, b, j],
            recv_sem=s_recv.at[slot, b, j], device_id=sibling, device_id_type=MESH,
        )

    fans = 4 if ring else half - 1

    def each_weight(condition, action):
        for b in range(nt):
            for slot in range(slots):
                @pl.when((b != t) & (slot < count(t)) & condition(b))
                def _():
                    action(b, slot)

    def half_copy(b, slot):
        ref = w_half(b, slot)
        return pltpu.make_async_remote_copy(
            src_ref=ref, dst_ref=ref, send_sem=s_send.at[slot, b, 0],
            recv_sem=s_recv.at[slot, b, 0], device_id=sibling, device_id_type=MESH,
        )

    def pass_half(b, slot):
        w_arrival(b, slot, True).wait_recv()
        half_copy(b, slot).start()

    def spread_first(b, slot):
        w_arrival(b, slot, False).wait_recv()
        for j in range(2 if ring else fans):
            fan_copy(b, slot, j).start()
        sibling_copy(b, slot, 0).start()

    def spread_second(b, slot):
        if ring:
            for j in range(2):
                fan_copy(b, slot, j).wait_recv()
                fan_copy(b, slot, 2 + j).start()
                sibling_copy(b, slot, 1 + j).start()

    def spread_third(b, slot):
        if ring:
            for j in (2, 3):
                fan_copy(b, slot, j).wait_recv()
            sibling_copy(b, slot, 3).start()
        else:
            for j in range(fans):
                fan_copy(b, slot, j).wait_recv()
                sibling_copy(b, slot, j + 1).start()

    def early(b):
        return beside_end(b)

    def late(b):
        return jnp.logical_not(beside_end(b))

    def inner_late(b):
        return late(b) & jnp.logical_not(is_end(b))

    def outer_late(b):
        return late(b) & is_end(b)

    def cols(kh):
        return pl.ds(kh * pair, pair)

    def part_copy(j, kh):
        other = (c + j) % nc
        return pltpu.make_async_remote_copy(
            src_ref=acc.at[at(other, query_rows), cols(kh)], dst_ref=part.at[j - 1, :, cols(kh)],
            send_sem=c_send.at[kh, j - 1], recv_sem=c_recv.at[kh, j - 1],
            device_id={"ctx": other}, device_id_type=MESH,
        )

    def z_copy(way, b, kh, e):
        ref = kz.at[b, e, :, cols(kh)]
        return pltpu.make_async_remote_copy(
            src_ref=ref, dst_ref=ref, send_sem=z_send.at[way, b, kh, e],
            recv_sem=z_recv.at[b, kh, e], device_id={"tensor": t + 1 - 2 * way},
            device_id_type=MESH,
        )

    def kp_at(other, kh):
        return kp.at[at(other, query_rows), cols(kh)]

    def kp_copy(j, kh):
        return pltpu.make_async_remote_copy(
            src_ref=kp_at(p, kh), dst_ref=kp_at(p, kh), send_sem=m_send.at[kh, j],
            recv_sem=m_recv.at[kh, j], device_id=same_core(half - 1 - j)[0],
            device_id_type=MESH,
        )

    def kp_sibling(j, kh):
        ref = kp_at(same_core(j)[1], kh)
        return pltpu.make_async_remote_copy(
            src_ref=ref, dst_ref=ref, send_sem=n_send.at[kh, j], recv_sem=n_recv.at[kh, j],
            device_id=sibling, device_id_type=MESH,
        )

    def dx_columns(b, slot):
        return pl.ds(pl.multiple_of((first(b) + slot) * unit, unit), unit)

    def dx_copy(r, e, slot):
        other = (t + r) % nt
        return pltpu.make_async_remote_copy(
            src_ref=dx_send.at[e, slot, at(other, half_rows), :],
            dst_ref=dx_ref.at[0, pl.ds(e * half_rows, half_rows), dx_columns(t, slot)],
            send_sem=d_send.at[e, slot, r - 1], recv_sem=d_recv.at[e, slot, r - 1],
            device_id={"tensor": other}, device_id_type=MESH,
        )

    def dx_arrival(r, e, slot):
        b = (t + nt - r) % nt
        ref = dx_ref.at[0, pl.ds(e * half_rows, half_rows), dx_columns(b, slot)]
        return pltpu.make_async_remote_copy(
            src_ref=ref, dst_ref=ref, send_sem=d_send.at[e, slot, r - 1],
            recv_sem=d_recv.at[e, slot, r - 1], device_id={"tensor": b}, device_id_type=MESH,
        )

    def dx_keep(e, slot):
        return pltpu.make_async_copy(
            dx_send.at[e, slot, at(t, half_rows), :],
            dx_ref.at[0, pl.ds(e * half_rows, half_rows), dx_columns(t, slot)],
            own_sem.at[1 + e, slot],
        )

    loads = [
        pltpu.make_async_copy(x_ref, x_rows(t), local_sem.at[0]),
        pltpu.make_async_copy(q_ref, q, local_sem.at[1]),
        pltpu.make_async_copy(o_ref, o, local_sem.at[2]),
        pltpu.make_async_copy(do_ref, do, local_sem.at[3]),
    ]
    weight_loads = []
    for kh in range(heads):
        for which, ref in enumerate((kw_ref, vw_ref)):
            weight_loads.append(pltpu.make_async_copy(
                ref.at[:, pl.ds(kh * hs, hs)], kwv.at[:, pl.ds(kh * pair + which * hs, hs)],
                local_sem.at[4 + 2 * kh + which],
            ))
    for copy in loads + weight_loads:
        copy.start()
    barrier = pltpu.get_barrier_semaphore()
    for r in range(1, nt):
        pl.semaphore_signal(
            barrier, inc=1, device_id={"tensor": (t + r) % nt}, device_id_type=MESH
        )
    for r in range(1, plane):
        other = (p + r) % plane
        pl.semaphore_signal(
            barrier, inc=1, device_id={"dp": other // nc, "ctx": other % nc}, device_id_type=MESH
        )
    pl.semaphore_wait(barrier, nt - 1 + plane - 1)

    for k in range(subs):
        for way in (0, 1):
            ok, copy = x_copy(way, 1, k, True)

            @pl.when(ok)
            def _():
                copy.start()

    to_plane(t, x_ref)
    for copy in loads + weight_loads:
        copy.wait()
    keep_copy(t).start()
    def own_wide(slot):
        return pltpu.make_async_copy(
            kwv.at[pl.ds(pl.multiple_of((first(t) + slot) * unit, unit), unit), :],
            wide.at[slot, t], own_sem.at[0, slot],
        )

    def each_own(action):
        for slot in range(slots):
            @pl.when(slot < count(t))
            def _():
                action(slot)

    each_own(lambda slot: own_wide(slot).start())
    send_weights(True, lambda to: True)

    def iota(axis):
        return lax.broadcasted_iota(jnp.int32, (BLK, BLK), axis)

    blocks = key_rows // BLK
    blocks_here = query_rows // BLK

    @pl.loop(0, blocks)
    def _(kb):
        key_owner = owner_ref[0, kb]
        key_seg = jnp.sum(
            jnp.where(iota(0) == iota(1), seg_ref[pl.ds(key_owner, 1), :], 0), axis=1,
            keepdims=True,
        )
        for qb in range(blocks_here):
            query_owner = owner_ref[0, c * blocks_here + qb]
            query_seg = seg_ref[pl.ds(query_owner, 1), :]
            withheld = 1 - table_ref[query_owner, key_owner]
            key_pos = iota(0) + (key_owner * BLK + withheld * (1 << 20))
            query_pos = iota(1) + query_owner * BLK
            same = (key_seg == 0) | (key_seg == query_seg)
            bias[at(kb, BLK), pl.ds(qb * BLK, BLK)] = jnp.where(
                (key_pos <= query_pos) & same, 0.0, -jnp.inf
            )

    @pl.loop(0, heads * groups)
    def _(i):
        head = at(i, hs)
        product = do[:, head].astype(FULL) * o[:, head].astype(FULL)
        corr[pl.ds(i, 1), :] = jnp.sum(product.T, axis=0, keepdims=True)

    depth = min(1024, width)

    def project(b):
        def step(i, total):
            return total + jnp.dot(
                g[at(b, rows), at(i, depth)], kwv[at(i, depth), :], preferred_element_type=FULL
            )

        total = lax.fori_loop(0, width // depth, step, jnp.zeros((rows, kv2), FULL))
        kv[pl.ds(pl.multiple_of(c * query_rows + b * rows, rows), rows), :] = total.astype(LOW)
        for j in range(1, nc):
            kv_copy(j, b).start()

    project(t)
    for s in range(1, nt):
        for k in range(subs):
            for way in (0, 1):
                b = t - s if way == 0 else t + s

                @pl.when((b >= 0) & (b < nt))
                def _():
                    x_copy(way, s, k, False)[1].wait_recv()

                if s < nt - 1:
                    ok, copy = x_copy(way, s + 1, k, False)

                    @pl.when(ok)
                    def _():
                        copy.start()

        for way in (0, 1):
            b = t - s if way == 0 else t + s

            @pl.when((b >= 0) & (b < nt))
            def _():
                project(b)
                keep_copy(b).start()

            @pl.when((b >= 0) & (b < nt) & (b != far))
            def _():
                to_plane(b, x_rows(b))

        if s == 1:
            send_weights(False, lambda to: (not to in (0, nt - 1)) & jnp.logical_not(is_end(t)))
        if s == nt // 2:
            send_weights(False, lambda to: (not to in (0, nt - 1)) & is_end(t))
            each_weight(inner_late, spread_first)

    send_weights(False, lambda to: is_end(t) & (to in (0, nt - 1)))
    for j in range(1, nc):
        for b in range(nt):
            kv_copy(j, b).wait_recv()

    acc[...] = jnp.zeros_like(acc)
    stack = math.gcd(groups, max(1, 2048 // key_rows))
    for kh in range(heads):
        key_cols = pl.ds(kh * pair, hs)
        value_cols = pl.ds(kh * pair + hs, hs)

        @pl.loop(0, groups // stack)
        def _(i):
            picked = [kh * groups + i * stack + n for n in range(stack)]
            lanes = [pl.ds(pl.multiple_of(head * hs, hs), hs) for head in picked]
            keys = kv[:, key_cols]
            queries = jnp.concatenate([q[:, head] for head in lanes], axis=0)
            grads = jnp.concatenate([do[:, head] for head in lanes], axis=0)
            scores = lax.dot_general(
                keys, queries, (((1,), (1,)), ((), ())), preferred_element_type=FULL
            )
            scores = scores * (scale * math.log2(math.e)) + jnp.concatenate(
                [bias[...]] * stack, axis=1
            )
            top = jnp.max(scores, axis=0, keepdims=True)
            weights = jnp.exp2(scores - top)
            probs = weights * (1.0 / jnp.sum(weights, axis=0, keepdims=True))
            acc[:, value_cols] += jnp.dot(
                probs.astype(LOW), grads, preferred_element_type=FULL
            )
            prob_grads = lax.dot_general(
                kv[:, value_cols], grads, (((1,), (1,)), ((), ())), preferred_element_type=FULL
            )
            corrections = jnp.concatenate([corr[pl.ds(head, 1), :] for head in picked], axis=1)
            score_grads = (probs * (prob_grads - corrections)).astype(LOW)
            acc[:, key_cols] += jnp.dot(score_grads, queries, preferred_element_type=FULL)
            query_grads = lax.dot_general(
                score_grads, keys, (((0,), (0,)), ((), ())), preferred_element_type=FULL
            )
            for n, head in enumerate(lanes):
                rows_n = slice(n * query_rows, (n + 1) * query_rows)
                qg_ref[0, :, head] = (query_grads[rows_n] * scale).astype(LOW)

        acc[:, key_cols] = acc[:, key_cols] * scale
        for j in range(1, nc):
            part_copy(j, kh).start()
        if kh == 0:
            each_weight(inner_late, spread_second)
            each_weight(outer_late, spread_first)

    send_weights(False, lambda to: jnp.logical_not(is_end(t)) & (to in (0, nt - 1)))

    each_weight(inner_late, spread_third)

    for kh in range(heads):
        for j in range(1, nc):
            part_copy(j, kh).wait_recv()
        total = acc[at(c, query_rows), cols(kh)]
        for j in range(1, nc):
            total = total + part[j - 1, :, cols(kh)]
        total = total.astype(LOW)
        kp[at(p, query_rows), cols(kh)] = total
        by_half = total.reshape(nt, 2, half_rows, pair)
        for e in range(2):
            kz[t, e, :, cols(kh)] = by_half[:, e].reshape(nt * half_rows, pair)
            for way in (0, 1):
                @pl.when(takes_part(t + 1 - 2 * way))
                def _():
                    z_copy(way, t, kh, e).start()

    each_weight(early, pass_half)
    each_weight(outer_late, spread_second)
    ends = (0, nt - 1)
    inner = [b for b in range(nt) if b not in ends]
    near = jnp.where(t < nt // 2, 0, nt - 1)
    tile = min(256, unit)

    def relay(b, kh, e):
        @pl.when((b != t) & takes_part(t))
        def _():
            z_copy(0, b, kh, e).wait_recv()

        @pl.when((b < t) & takes_part(t) & takes_part(t + 1))
        def _():
            z_copy(0, b, kh, e).start()

        @pl.when((b > t) & takes_part(t) & takes_part(t - 1))
        def _():
            z_copy(1, b, kh, e).start()

    def product(left, slot, b, columns):
        return lax.dot_general(
            left, wide[slot, b, columns, :], (((1,), (1,)), ((), ())),
            preferred_element_type=FULL,
        )

    for b in sorted(inner, key=lambda b: abs(2 * b - nt + 1)):
        for kh in range(heads):
            for e in range(2):
                relay(b, kh, e)
    each_own(lambda slot: own_wide(slot).wait())

    def spread_done(b, slot):
        for j in range(half):
            sibling_copy(b, slot, j).wait_recv()

    def input_grads_inner(slot):
        @pl.loop(0, unit // tile)
        def _(n):
            columns = at(n, tile)
            out = None
            for b in inner:
                term = product(kz[b].reshape(query_rows, kv2), slot, b, columns)
                out = term if out is None else out + term
            dx_sum[slot, :, columns] = out

    def input_grads_near(slot):
        @pl.loop(0, unit // tile)
        def _(n):
            columns = at(n, tile)
            dx_sum[slot, :, columns] += product(
                kz[near].reshape(query_rows, kv2), slot, near, columns
            )

    each_weight(inner_late, spread_done)
    each_own(input_grads_inner)
    for kh in range(heads):
        for e in range(2):
            relay(near, kh, e)
    each_weight(early, lambda b, slot: half_copy(b, slot).wait_recv())
    if ring:
        each_weight(outer_late, spread_third)
        each_own(input_grads_near)
        each_weight(outer_late, spread_done)
    else:
        each_weight(outer_late, spread_third)
        each_weight(outer_late, spread_done)
        each_own(input_grads_near)
    for kh in range(heads):
        for j in range(half - 1):
            kp_copy(j, kh).start()
        kp_sibling(0, kh).start()
    to_plane(far, x_rows(far))

    for e in range(2):
        for kh in range(heads):
            relay(far, kh, e)

        def input_grads(slot):
            @pl.loop(0, unit // tile)
            def _(n):
                columns = at(n, tile)
                part_rows = pl.ds(e * nt * half_rows, nt * half_rows)
                dx_send[e, slot, :, columns] = (
                    dx_sum[slot, part_rows, columns] + product(kz[far, e], slot, far, columns)
                ).astype(LOW)

            for r in range(1, nt):
                dx_copy(r, e, slot).start()
            dx_keep(e, slot).start()

        each_own(input_grads)

    for b in range(nt):
        for r in range(1, plane):
            plane_copy(b, r, x_ref).wait_recv()
        keep_copy(b).wait()
    for kh in range(heads):
        for j in range(half - 1):
            kp_copy(j, kh).wait_recv()
            kp_sibling(j + 1, kh).start()
    for kh in range(heads):
        for j in range(half):
            kp_sibling(j, kh).wait_recv()
    step_width = min(256, slice_width)
    plane_rows = xc.reshape(plane * nt * rows, slice_width)

    @pl.loop(0, slice_width // step_width)
    def _(m):
        columns = at(m, step_width)
        out = lax.dot_general(
            plane_rows[:, columns], kp[...], (((0,), (0,)), ((), ())),
            preferred_element_type=FULL,
        ).astype(LOW)
        for kh in range(heads):
            dkw_ref[columns, pl.ds(kh * hs, hs)] = out[:, kh * pair:kh * pair + hs]
            dvw_ref[columns, pl.ds(kh * hs, hs)] = out[:, kh * pair + hs:(kh + 1) * pair]

    for s in range(1, nt):
        for k in range(subs):
            for way in (0, 1):
                ok, copy = x_copy(way, s, k, s == 1)

                @pl.when(ok)
                def _():
                    copy.wait_send()

    for direct in (False, True):
        each_target(direct, lambda copy, to: copy.wait_send())

    def spread_sent(b, slot):
        for j in range(fans):
            fan_copy(b, slot, j).wait_send()
        for j in range(half):
            sibling_copy(b, slot, j).wait_send()

    each_weight(late, spread_sent)
    each_weight(early, lambda b, slot: half_copy(b, slot).wait_send())
    for b in range(nt):
        for r in range(1, plane):
            plane_copy(b, r, x_ref).wait_send()
        for j in range(1, nc):
            kv_copy(j, b).wait_send()
    for kh in range(heads):
        for j in range(1, nc):
            part_copy(j, kh).wait_send()
        for j in range(half - 1):
            kp_copy(j, kh).wait_send()
        for j in range(half):
            kp_sibling(j, kh).wait_send()
        for e in range(2):
            for b in range(nt):
                sent_it = (b == t) | takes_part(t)

                @pl.when((b <= t) & sent_it & takes_part(t + 1))
                def _():
                    z_copy(0, b, kh, e).wait_send()

                @pl.when((b >= t) & sent_it & takes_part(t - 1))
                def _():
                    z_copy(1, b, kh, e).wait_send()

    for e in range(2):
        def sent(slot):
            for r in range(1, nt):
                dx_copy(r, e, slot).wait_send()
            dx_keep(e, slot).wait()

        each_own(sent)
        for r in range(1, nt):
            for slot in range(slots):
                @pl.when(slot < count((t + nt - r) % nt))
                def _():
                    dx_arrival(r, e, slot).wait_recv()


def copy_kernel(parts, count, *refs):
    sources, targets, held = refs[:count], refs[count:2 * count], refs[2 * count:3 * count]
    in_sem, out_sem = refs[3 * count:]
    inward, outward = [], []
    for i in range(count):
        size = sources[i].shape[-2] // parts
        for k in range(parts):
            index = (0,) * (len(sources[i].shape) - 2) + (pl.ds(k * size, size),)
            inward.append(pltpu.make_async_copy(
                sources[i].at[index], held[i].at[index], in_sem.at[i, k]
            ))
            outward.append(pltpu.make_async_copy(
                held[i].at[index], targets[i].at[index], out_sem.at[i, k]
            ))
    for copy in inward:
        copy.start()
    for arrived, copy in zip(inward, outward):
        arrived.wait()
        copy.start()
    for copy in outward:
        copy.wait()


def to_outputs(arrays):
    hbm = pl.BlockSpec(memory_space=pltpu.HBM)
    parts = 2
    count = len(arrays)
    dma = pltpu.SemaphoreType.DMA
    return pl.pallas_call(
        functools.partial(copy_kernel, parts, count),
        out_shape=tuple(jax.ShapeDtypeStruct(a.shape, a.dtype) for a in arrays),
        in_specs=[hbm] * count,
        out_specs=[hbm] * count,
        scratch_shapes=[pltpu.VMEM(a.shape, a.dtype) for a in arrays]
        + [dma((count, parts)), dma((count, parts))],
    )(*arrays)


def per_device(
    layer_input,
    queries,
    forward_output,
    attention_output_gradient,
    key_weight,
    value_projection_weight,
    segment,
    block_table,
    block_owner,
):
    nt, nd, nc = lax.axis_size("tensor"), lax.axis_size("dp"), lax.axis_size("ctx")
    plane = nd * nc
    half = plane // 2
    rows, width = layer_input.shape[1:]
    query_rows, query_width = queries.shape[1:]
    kv = key_weight.shape[1]
    heads = kv // HEAD_SIZE
    groups = query_width // kv
    blocks = block_owner.shape[1]
    key_rows = nc * query_rows
    end_units, mid_units = UNITS if nt == 4 else (1, 1)
    unit = width // (2 * end_units + (nt - 2) * mid_units)
    slots = max(end_units, mid_units)
    fans = 4 if nt == 4 and nc == 2 and half == 4 and end_units == 0 else half - 1
    slice_width = width // plane
    subs = min(4, rows // 16)
    dma = pltpu.SemaphoreType.DMA
    hbm = pl.BlockSpec(memory_space=pltpu.HBM)
    vmem = pl.BlockSpec(memory_space=pltpu.VMEM)
    smem = pl.BlockSpec(memory_space=pltpu.SMEM)
    query_grad, input_grad, key_weight_grad, value_weight_grad = pl.pallas_call(
        functools.partial(grads_kernel, nt, nd, nc, heads, groups, subs, end_units, mid_units),
        out_shape=(
            jax.ShapeDtypeStruct((1, query_rows, query_width), LOW),
            jax.ShapeDtypeStruct((1, rows, width), LOW),
            jax.ShapeDtypeStruct((slice_width, kv), LOW),
            jax.ShapeDtypeStruct((slice_width, kv), LOW),
        ),
        in_specs=[hbm] * 6 + [vmem, smem, smem],
        out_specs=[vmem] * 4,
        scratch_shapes=[
            pltpu.VMEM((nt * rows, width), LOW),
            pltpu.VMEM((width, 2 * kv), LOW),
            pltpu.VMEM((slots, nt, unit, 2 * kv), LOW),
            pltpu.VMEM((plane, nt, rows, slice_width), LOW),
            pltpu.VMEM((query_rows, query_width), LOW),
            pltpu.VMEM((query_rows, query_width), LOW),
            pltpu.VMEM((query_rows, query_width), LOW),
            pltpu.VMEM((key_rows, 2 * kv), LOW),
            pltpu.VMEM((key_rows, query_rows), FULL),
            pltpu.VMEM((heads * groups, query_rows), FULL),
            pltpu.VMEM((key_rows, 2 * kv), FULL),
            pltpu.VMEM((nc - 1, query_rows, 2 * kv), FULL),
            pltpu.VMEM((nt, 2, query_rows // 2, 2 * kv), LOW),
            pltpu.VMEM((plane * query_rows, 2 * kv), LOW),
            pltpu.VMEM((slots, query_rows, unit), FULL),
            pltpu.VMEM((2, slots, query_rows // 2, unit), LOW),
            dma((2, nt - 1, subs)), dma((2, nt - 1, subs)),
            dma((nt, slots)), dma((nt, slots)),
            dma((nt, plane - 1)), dma((nt, plane - 1)),
            dma((slots, nt, fans)), dma((slots, nt, fans)),
            dma((slots, nt, half)), dma((slots, nt, half)),
            dma((heads, half - 1)), dma((heads, half - 1)),
            dma((heads, half)), dma((heads, half)),
            dma((nc - 1, nt)), dma((nc - 1, nt)),
            dma((heads, nc - 1)), dma((heads, nc - 1)),
            dma((2, nt, heads, 2)), dma((nt, heads, 2)),
            dma((2, slots, nt - 1)), dma((2, slots, nt - 1)),
            dma((4 + 2 * heads,)), dma((3, slots)), dma((nt,)),
        ],
        compiler_params=pltpu.CompilerParams(
            collective_id=0, has_side_effects=True, vmem_limit_bytes=60 << 20
        ),
    )(
        layer_input[0], queries[0], forward_output[0], attention_output_gradient[0],
        key_weight, value_projection_weight,
        segment.reshape(blocks, BLK), block_table[0], block_owner,
    )
    return to_outputs((query_grad, input_grad, key_weight_grad, value_weight_grad))


def solution(mesh):
    in_specs = (
        P("dp", ("ctx", "tensor"), None),
        P("dp", "ctx", "tensor"),
        P("dp", "ctx", "tensor"),
        P("dp", "ctx", "tensor"),
        P(None, "tensor"),
        P(None, "tensor"),
        P("dp", None),
        P("dp", None, None),
        P("dp", None),
    )
    out_specs = (
        P("dp", "ctx", "tensor"),
        P("dp", ("ctx", "tensor"), None),
        P(("dp", "ctx"), "tensor"),
        P(("dp", "ctx"), "tensor"),
    )
    return jax.shard_map(
        per_device, mesh=mesh, in_specs=in_specs, out_specs=out_specs, check_vma=False
    )
```

```python
import functools
import math

import jax
import jax.numpy as jnp
from jax import lax
from jax.experimental import pallas as pl
from jax.experimental.pallas import tpu as pltpu
from jax.sharding import PartitionSpec as P

HEAD_SIZE = 128
BLK = 128
UNITS = (0, 4)

MESH = pl.DeviceIdType.MESH
LOW = jnp.bfloat16
FULL = jnp.float32


def grads_kernel(
    nt, nd, nc, heads, groups, subs, end_units, mid_units,
    x_ref, q_ref, o_ref, do_ref, kw_ref, vw_ref, seg_ref, table_ref, owner_ref,
    qg_ref, dx_ref, dkw_ref, dvw_ref,
    g, kwv, wide, xc, q, o, do, kv, bias, corr, acc, part, kz, kp, dx_sum, dx_send,
    x_send, x_recv, w_send, w_recv, p_send, p_recv, f_send, f_recv, s_send, s_recv,
    m_send, m_recv, n_send, n_recv, k_send, k_recv, c_send, c_recv, z_send, z_recv, d_send, d_recv,
    local_sem, own_sem, keep_sem,
):
    t = lax.axis_index("tensor")
    d = lax.axis_index("dp")
    c = lax.axis_index("ctx")
    plane = nd * nc
    half = plane // 2
    p = d * nc + c
    h = (d // 2) * nc + c
    core = d % 2
    rows, width = x_ref.shape
    kv2 = kwv.shape[1]
    unit = wide.shape[2]
    slots = wide.shape[0]
    piece = unit // plane
    slice_width = width // plane
    query_rows = nt * rows
    key_rows = nc * query_rows
    sub_rows = rows // subs
    hs = HEAD_SIZE
    pair = 2 * hs
    half_rows = rows // 2
    scale = 1.0 / math.sqrt(hs)

    def at(i, size):
        return pl.ds(pl.multiple_of(i * size, size), size)

    def is_end(b):
        return (b == 0) | (b == nt - 1)

    def count(b):
        return jnp.where(is_end(b), end_units, mid_units)

    def first(b):
        return jnp.where(b == 0, 0, end_units + (b - 1) * mid_units)

    def beside_end(b):
        return ring & is_end(b) & ((b == t + 1) | (b == t - 1))

    def takes_part(b):
        return (b >= 0) & (b < nt) & (count(b) > 0)

    far = jnp.where(t < nt // 2, nt - 1, 0)
    ring = nt == 4 and nc == 2 and half == 4 and end_units == 0

    def x_rows(b):
        return g.at[at(b, rows), :]

    def x_copy(way, s, k, first):
        step = 1 if way == 0 else -1
        b = t - step * (s - 1)
        target = t + step
        ok = (target >= 0) & (target < nt) & (b >= 0) & (b < nt)
        dst = g.at[pl.ds(pl.multiple_of(b * rows + k * sub_rows, sub_rows), sub_rows), :]
        src = x_ref.at[pl.ds(k * sub_rows, sub_rows), :] if first else dst
        return ok, pltpu.make_async_remote_copy(
            src_ref=src, dst_ref=dst, send_sem=x_send.at[way, s - 1, k],
            recv_sem=x_recv.at[way, s - 1, k], device_id={"tensor": target}, device_id_type=MESH,
        )

    def w_copy(to, slot, direct):
        share, size = (core, unit // 2) if direct else (p, piece)
        begin = (first(to) + slot) * unit + share * size
        return pltpu.make_async_remote_copy(
            src_ref=kwv.at[pl.ds(pl.multiple_of(begin, size), size), :],
            dst_ref=wide.at[slot, t, at(share, size), :],
            send_sem=w_send.at[to, slot], recv_sem=w_recv.at[t, slot],
            device_id={"tensor": to}, device_id_type=MESH,
        )

    def w_half(b, slot):
        return wide.at[slot, b, at(core, unit // 2), :]

    def w_arrival(b, slot, direct):
        ref = w_half(b, slot) if direct else wide.at[slot, b, at(p, piece), :]
        return pltpu.make_async_remote_copy(
            src_ref=ref, dst_ref=ref, send_sem=w_send.at[b, slot], recv_sem=w_recv.at[b, slot],
            device_id={"tensor": b}, device_id_type=MESH,
        )

    def each_target(direct, action):
        for slot in range(slots):
            for to in range(nt):
                if slot < (end_units if to in (0, nt - 1) else mid_units):
                    beside = is_end(t) & ((t == to + 1) | (t == to - 1)) & ring
                    good = beside if direct else (t != to) & jnp.logical_not(beside)

                    @pl.when(good)
                    def _():
                        action(w_copy(to, slot, direct), to)

    def send_weights(direct, condition):
        def send(copy, to):
            @pl.when(condition(to))
            def _():
                copy.start()

        each_target(direct, send)

    def plane_copy(b, r, source):
        other = (p + r) % plane
        return pltpu.make_async_remote_copy(
            src_ref=source.at[:, at(other, slice_width)], dst_ref=xc.at[p, b],
            send_sem=p_send.at[b, r - 1], recv_sem=p_recv.at[b, r - 1],
            device_id={"dp": other // nc, "ctx": other % nc}, device_id_type=MESH,
        )

    def to_plane(b, source):
        for r in range(1, plane):
            plane_copy(b, r, source).start()

    def keep_copy(b):
        return pltpu.make_async_copy(
            x_rows(b).at[:, at(p, slice_width)], xc.at[p, b], keep_sem.at[b]
        )

    def kv_copy(j, b):
        own = kv.at[pl.ds(pl.multiple_of(c * query_rows + b * rows, rows), rows), :]
        return pltpu.make_async_remote_copy(
            src_ref=own, dst_ref=own, send_sem=k_send.at[j - 1, b], recv_sem=k_recv.at[j - 1, b],
            device_id={"ctx": (c + j) % nc}, device_id_type=MESH,
        )

    def same_core(j):
        hh = (h + half - j) % half
        return {"dp": (hh // nc) * 2 + core, "ctx": hh % nc}, (
            ((hh // nc) * 2 + core) * nc + hh % nc
        )

    sibling = {"dp": d + 1 - 2 * core}

    def wide_at(slot, b, other, lo=0, size=None):
        return wide.at[
            slot, b, pl.ds(pl.multiple_of(other * piece + lo, 16), size or piece), :
        ]

    beside_x = d * nc + (c + 1) % nc
    beside_y = ((d + 2) % nd) * nc + c
    across = ((d + 2) % nd) * nc + (c + 1) % nc

    def fan_copy(b, slot, j):
        if ring:
            lower = piece // 2
            ref, to = (
                (wide_at(slot, b, p), {"ctx": (c + 1) % nc}),
                (wide_at(slot, b, p), {"dp": (d + 2) % nd}),
                (wide_at(slot, b, beside_x, 0, lower), {"dp": (d + 2) % nd}),
                (wide_at(slot, b, beside_y, lower, lower), {"ctx": (c + 1) % nc}),
            )[j]
        else:
            ref, to = wide_at(slot, b, p), same_core(half - 1 - j)[0]
        return pltpu.make_async_remote_copy(
            src_ref=ref, dst_ref=ref, send_sem=f_send.at[slot, b, j],
            recv_sem=f_recv.at[slot, b, j], device_id=to, device_id_type=MESH,
        )

    def sibling_copy(b, slot, j):
        if ring:
            other = (p, beside_x, beside_y, across)[j]
        else:
            other = same_core(j)[1]
        ref = wide_at(slot, b, other)
        return pltpu.make_async_remote_copy(
            src_ref=ref, dst_ref=ref, send_sem=s_send.at[slot, b, j],
            recv_sem=s_recv.at[slot, b, j], device_id=sibling, device_id_type=MESH,
        )

    fans = 4 if ring else half - 1

    def each_weight(condition, action):
        for b in range(nt):
            for slot in range(slots):
                @pl.when((b != t) & (slot < count(t)) & condition(b))
                def _():
                    action(b, slot)

    def half_copy(b, slot):
        ref = w_half(b, slot)
        return pltpu.make_async_remote_copy(
            src_ref=ref, dst_ref=ref, send_sem=s_send.at[slot, b, 0],
            recv_sem=s_recv.at[slot, b, 0], device_id=sibling, device_id_type=MESH,
        )

    def pass_half(b, slot):
        w_arrival(b, slot, True).wait_recv()
        half_copy(b, slot).start()

    def spread_first(b, slot):
        w_arrival(b, slot, False).wait_recv()
        for j in range(2 if ring else fans):
            fan_copy(b, slot, j).start()
        sibling_copy(b, slot, 0).start()

    def spread_second(b, slot):
        if ring:
            for j in range(2):
                fan_copy(b, slot, j).wait_recv()
                fan_copy(b, slot, 2 + j).start()
                sibling_copy(b, slot, 1 + j).start()

    def spread_third(b, slot):
        if ring:
            for j in (2, 3):
                fan_copy(b, slot, j).wait_recv()
            sibling_copy(b, slot, 3).start()
        else:
            for j in range(fans):
                fan_copy(b, slot, j).wait_recv()
                sibling_copy(b, slot, j + 1).start()

    def early(b):
        return beside_end(b)

    def late(b):
        return jnp.logical_not(beside_end(b))

    def inner_late(b):
        return late(b) & jnp.logical_not(is_end(b))

    def outer_late(b):
        return late(b) & is_end(b)

    def cols(kh):
        return pl.ds(kh * pair, pair)

    def part_copy(j, kh):
        other = (c + j) % nc
        return pltpu.make_async_remote_copy(
            src_ref=acc.at[at(other, query_rows), cols(kh)], dst_ref=part.at[j - 1, :, cols(kh)],
            send_sem=c_send.at[kh, j - 1], recv_sem=c_recv.at[kh, j - 1],
            device_id={"ctx": other}, device_id_type=MESH,
        )

    def z_copy(way, b, kh, e):
        ref = kz.at[b, e, :, cols(kh)]
        return pltpu.make_async_remote_copy(
            src_ref=ref, dst_ref=ref, send_sem=z_send.at[way, b, kh, e],
            recv_sem=z_recv.at[b, kh, e], device_id={"tensor": t + 1 - 2 * way},
            device_id_type=MESH,
        )

    def kp_at(other, kh):
        return kp.at[at(other, query_rows), cols(kh)]

    def kp_copy(j, kh):
        return pltpu.make_async_remote_copy(
            src_ref=kp_at(p, kh), dst_ref=kp_at(p, kh), send_sem=m_send.at[kh, j],
            recv_sem=m_recv.at[kh, j], device_id=same_core(half - 1 - j)[0],
            device_id_type=MESH,
        )

    def kp_sibling(j, kh):
        ref = kp_at(same_core(j)[1], kh)
        return pltpu.make_async_remote_copy(
            src_ref=ref, dst_ref=ref, send_sem=n_send.at[kh, j], recv_sem=n_recv.at[kh, j],
            device_id=sibling, device_id_type=MESH,
        )

    def dx_columns(b, slot):
        return pl.ds(pl.multiple_of((first(b) + slot) * unit, unit), unit)

    def dx_copy(r, e, slot):
        other = (t + r) % nt
        return pltpu.make_async_remote_copy(
            src_ref=dx_send.at[e, slot, at(other, half_rows), :],
            dst_ref=dx_ref.at[0, pl.ds(e * half_rows, half_rows), dx_columns(t, slot)],
            send_sem=d_send.at[e, slot, r - 1], recv_sem=d_recv.at[e, slot, r - 1],
            device_id={"tensor": other}, device_id_type=MESH,
        )

    def dx_arrival(r, e, slot):
        b = (t + nt - r) % nt
        ref = dx_ref.at[0, pl.ds(e * half_rows, half_rows), dx_columns(b, slot)]
        return pltpu.make_async_remote_copy(
            src_ref=ref, dst_ref=ref, send_sem=d_send.at[e, slot, r - 1],
            recv_sem=d_recv.at[e, slot, r - 1], device_id={"tensor": b}, device_id_type=MESH,
        )

    def dx_keep(e, slot):
        return pltpu.make_async_copy(
            dx_send.at[e, slot, at(t, half_rows), :],
            dx_ref.at[0, pl.ds(e * half_rows, half_rows), dx_columns(t, slot)],
            own_sem.at[1 + e, slot],
        )

    loads = [
        pltpu.make_async_copy(x_ref, x_rows(t), local_sem.at[0]),
        pltpu.make_async_copy(q_ref, q, local_sem.at[1]),
        pltpu.make_async_copy(o_ref, o, local_sem.at[2]),
        pltpu.make_async_copy(do_ref, do, local_sem.at[3]),
    ]
    weight_loads = []
    for kh in range(heads):
        for which, ref in enumerate((kw_ref, vw_ref)):
            weight_loads.append(pltpu.make_async_copy(
                ref.at[:, pl.ds(kh * hs, hs)], kwv.at[:, pl.ds(kh * pair + which * hs, hs)],
                local_sem.at[4 + 2 * kh + which],
            ))
    for copy in loads + weight_loads:
        copy.start()
    barrier = pltpu.get_barrier_semaphore()
    for r in range(1, nt):
        pl.semaphore_signal(
            barrier, inc=1, device_id={"tensor": (t + r) % nt}, device_id_type=MESH
        )
    for r in range(1, plane):
        other = (p + r) % plane
        pl.semaphore_signal(
            barrier, inc=1, device_id={"dp": other // nc, "ctx": other % nc}, device_id_type=MESH
        )
    pl.semaphore_wait(barrier, nt - 1 + plane - 1)

    for k in range(subs):
        for way in (0, 1):
            ok, copy = x_copy(way, 1, k, True)

            @pl.when(ok)
            def _():
                copy.start()

    to_plane(t, x_ref)
    for copy in loads + weight_loads:
        copy.wait()
    keep_copy(t).start()
    def own_wide(slot):
        return pltpu.make_async_copy(
            kwv.at[pl.ds(pl.multiple_of((first(t) + slot) * unit, unit), unit), :],
            wide.at[slot, t], own_sem.at[0, slot],
        )

    def each_own(action):
        for slot in range(slots):
            @pl.when(slot < count(t))
            def _():
                action(slot)

    each_own(lambda slot: own_wide(slot).start())
    send_weights(True, lambda to: True)

    def iota(axis):
        return lax.broadcasted_iota(jnp.int32, (BLK, BLK), axis)

    blocks = key_rows // BLK
    blocks_here = query_rows // BLK

    @pl.loop(0, blocks)
    def _(kb):
        key_owner = owner_ref[0, kb]
        key_seg = jnp.sum(
            jnp.where(iota(0) == iota(1), seg_ref[pl.ds(key_owner, 1), :], 0), axis=1,
            keepdims=True,
        )
        for qb in range(blocks_here):
            query_owner = owner_ref[0, c * blocks_here + qb]
            query_seg = seg_ref[pl.ds(query_owner, 1), :]
            withheld = 1 - table_ref[query_owner, key_owner]
            key_pos = iota(0) + (key_owner * BLK + withheld * (1 << 20))
            query_pos = iota(1) + query_owner * BLK
            same = (key_seg == 0) | (key_seg == query_seg)
            bias[at(kb, BLK), pl.ds(qb * BLK, BLK)] = jnp.where(
                (key_pos <= query_pos) & same, 0.0, -jnp.inf
            )

    @pl.loop(0, heads * groups)
    def _(i):
        head = at(i, hs)
        product = do[:, head].astype(FULL) * o[:, head].astype(FULL)
        corr[pl.ds(i, 1), :] = jnp.sum(product.T, axis=0, keepdims=True)

    depth = min(1024, width)

    def project(b):
        def step(i, total):
            return total + jnp.dot(
                g[at(b, rows), at(i, depth)], kwv[at(i, depth), :], preferred_element_type=FULL
            )

        total = lax.fori_loop(0, width // depth, step, jnp.zeros((rows, kv2), FULL))
        kv[pl.ds(pl.multiple_of(c * query_rows + b * rows, rows), rows), :] = total.astype(LOW)
        for j in range(1, nc):
            kv_copy(j, b).start()

    project(t)
    for s in range(1, nt):
        for k in range(subs):
            for way in (0, 1):
                b = t - s if way == 0 else t + s

                @pl.when((b >= 0) & (b < nt))
                def _():
                    x_copy(way, s, k, False)[1].wait_recv()

                if s < nt - 1:
                    ok, copy = x_copy(way, s + 1, k, False)

                    @pl.when(ok)
                    def _():
                        copy.start()

        for way in (0, 1):
            b = t - s if way == 0 else t + s

            @pl.when((b >= 0) & (b < nt))
            def _():
                project(b)
                keep_copy(b).start()

            @pl.when((b >= 0) & (b < nt) & (b != far))
            def _():
                to_plane(b, x_rows(b))

        if s == 1:
            send_weights(False, lambda to: (not to in (0, nt - 1)) & jnp.logical_not(is_end(t)))
            send_weights(False, lambda to: (not to in (0, nt - 1)) & is_end(t))
        if s == nt // 2:
            each_weight(inner_late, spread_first)

    send_weights(False, lambda to: is_end(t) & (to in (0, nt - 1)))
    for j in range(1, nc):
        for b in range(nt):
            kv_copy(j, b).wait_recv()

    acc[...] = jnp.zeros_like(acc)
    stack = math.gcd(groups, max(1, 2048 // key_rows))
    for kh in range(heads):
        key_cols = pl.ds(kh * pair, hs)
        value_cols = pl.ds(kh * pair + hs, hs)

        @pl.loop(0, groups // stack)
        def _(i):
            picked = [kh * groups + i * stack + n for n in range(stack)]
            lanes = [pl.ds(pl.multiple_of(head * hs, hs), hs) for head in picked]
            keys = kv[:, key_cols]
            queries = jnp.concatenate([q[:, head] for head in lanes], axis=0)
            grads = jnp.concatenate([do[:, head] for head in lanes], axis=0)
            scores = lax.dot_general(
                keys, queries, (((1,), (1,)), ((), ())), preferred_element_type=FULL
            )
            scores = scores * (scale * math.log2(math.e)) + jnp.concatenate(
                [bias[...]] * stack, axis=1
            )
            top = jnp.max(scores, axis=0, keepdims=True)
            weights = jnp.exp2(scores - top)
            probs = weights * (1.0 / jnp.sum(weights, axis=0, keepdims=True))
            acc[:, value_cols] += jnp.dot(
                probs.astype(LOW), grads, preferred_element_type=FULL
            )
            prob_grads = lax.dot_general(
                kv[:, value_cols], grads, (((1,), (1,)), ((), ())), preferred_element_type=FULL
            )
            corrections = jnp.concatenate([corr[pl.ds(head, 1), :] for head in picked], axis=1)
            score_grads = (probs * (prob_grads - corrections)).astype(LOW)
            acc[:, key_cols] += jnp.dot(score_grads, queries, preferred_element_type=FULL)
            query_grads = lax.dot_general(
                score_grads, keys, (((0,), (0,)), ((), ())), preferred_element_type=FULL
            )
            for n, head in enumerate(lanes):
                rows_n = slice(n * query_rows, (n + 1) * query_rows)
                qg_ref[0, :, head] = (query_grads[rows_n] * scale).astype(LOW)

        acc[:, key_cols] = acc[:, key_cols] * scale
        for j in range(1, nc):
            part_copy(j, kh).start()
        if kh == 0:
            each_weight(inner_late, spread_second)
            each_weight(outer_late, spread_first)

    send_weights(False, lambda to: jnp.logical_not(is_end(t)) & (to in (0, nt - 1)))

    each_weight(inner_late, spread_third)
    each_weight(outer_late, spread_second)

    for kh in range(heads):
        for j in range(1, nc):
            part_copy(j, kh).wait_recv()
        total = acc[at(c, query_rows), cols(kh)]
        for j in range(1, nc):
            total = total + part[j - 1, :, cols(kh)]
        total = total.astype(LOW)
        kp[at(p, query_rows), cols(kh)] = total
        by_half = total.reshape(nt, 2, half_rows, pair)
        for e in range(2):
            kz[t, e, :, cols(kh)] = by_half[:, e].reshape(nt * half_rows, pair)
            for way in (0, 1):
                @pl.when(takes_part(t + 1 - 2 * way))
                def _():
                    z_copy(way, t, kh, e).start()

    each_weight(early, pass_half)
    for kh in range(heads):
        for j in range(half - 1):
            kp_copy(j, kh).start()
        kp_sibling(0, kh).start()
    ends = (0, nt - 1)
    inner = [b for b in range(nt) if b not in ends]
    near = jnp.where(t < nt // 2, 0, nt - 1)
    tile = min(256, unit)

    def relay(b, kh, e):
        @pl.when((b != t) & takes_part(t))
        def _():
            z_copy(0, b, kh, e).wait_recv()

        @pl.when((b < t) & takes_part(t) & takes_part(t + 1))
        def _():
            z_copy(0, b, kh, e).start()

        @pl.when((b > t) & takes_part(t) & takes_part(t - 1))
        def _():
            z_copy(1, b, kh, e).start()

    def product(left, slot, b, columns):
        return lax.dot_general(
            left, wide[slot, b, columns, :], (((1,), (1,)), ((), ())),
            preferred_element_type=FULL,
        )

    for b in sorted(inner, key=lambda b: abs(2 * b - nt + 1)):
        for kh in range(heads):
            for e in range(2):
                relay(b, kh, e)
    each_own(lambda slot: own_wide(slot).wait())

    def spread_done(b, slot):
        for j in range(half):
            sibling_copy(b, slot, j).wait_recv()

    def input_grads_inner(slot):
        @pl.loop(0, unit // tile)
        def _(n):
            columns = at(n, tile)
            out = None
            for b in inner:
                term = product(kz[b].reshape(query_rows, kv2), slot, b, columns)
                out = term if out is None else out + term
            dx_sum[slot, :, columns] = out

    each_weight(inner_late, spread_done)
    each_own(input_grads_inner)
    for kh in range(heads):
        for e in range(2):
            relay(near, kh, e)
    each_weight(early, lambda b, slot: half_copy(b, slot).wait_recv())
    if ring:
        each_weight(outer_late, spread_third)
        each_weight(outer_late, spread_done)
    else:
        each_weight(outer_late, spread_third)
        each_weight(outer_late, spread_done)
    to_plane(far, x_rows(far))

    for e in range(2):
        for kh in range(heads):
            relay(far, kh, e)

        def input_grads(slot):
            @pl.loop(0, unit // tile)
            def _(n):
                columns = at(n, tile)
                part_rows = pl.ds(e * nt * half_rows, nt * half_rows)
                dx_send[e, slot, :, columns] = (
                    dx_sum[slot, part_rows, columns] + product(kz[near, e], slot, near, columns)
                    + product(kz[far, e], slot, far, columns)
                ).astype(LOW)

            for r in range(1, nt):
                dx_copy(r, e, slot).start()
            dx_keep(e, slot).start()

        each_own(input_grads)

    for b in range(nt):
        for r in range(1, plane):
            plane_copy(b, r, x_ref).wait_recv()
        keep_copy(b).wait()
    for kh in range(heads):
        for j in range(half - 1):
            kp_copy(j, kh).wait_recv()
            kp_sibling(j + 1, kh).start()
    for kh in range(heads):
        for j in range(half):
            kp_sibling(j, kh).wait_recv()
    step_width = min(256, slice_width)
    plane_rows = xc.reshape(plane * nt * rows, slice_width)

    @pl.loop(0, slice_width // step_width)
    def _(m):
        columns = at(m, step_width)
        out = lax.dot_general(
            plane_rows[:, columns], kp[...], (((0,), (0,)), ((), ())),
            preferred_element_type=FULL,
        ).astype(LOW)
        for kh in range(heads):
            dkw_ref[columns, pl.ds(kh * hs, hs)] = out[:, kh * pair:kh * pair + hs]
            dvw_ref[columns, pl.ds(kh * hs, hs)] = out[:, kh * pair + hs:(kh + 1) * pair]

    for s in range(1, nt):
        for k in range(subs):
            for way in (0, 1):
                ok, copy = x_copy(way, s, k, s == 1)

                @pl.when(ok)
                def _():
                    copy.wait_send()

    for direct in (False, True):
        each_target(direct, lambda copy, to: copy.wait_send())

    def spread_sent(b, slot):
        for j in range(fans):
            fan_copy(b, slot, j).wait_send()
        for j in range(half):
            sibling_copy(b, slot, j).wait_send()

    each_weight(late, spread_sent)
    each_weight(early, lambda b, slot: half_copy(b, slot).wait_send())
    for b in range(nt):
        for r in range(1, plane):
            plane_copy(b, r, x_ref).wait_send()
        for j in range(1, nc):
            kv_copy(j, b).wait_send()
    for kh in range(heads):
        for j in range(1, nc):
            part_copy(j, kh).wait_send()
        for j in range(half - 1):
            kp_copy(j, kh).wait_send()
        for j in range(half):
            kp_sibling(j, kh).wait_send()
        for e in range(2):
            for b in range(nt):
                sent_it = (b == t) | takes_part(t)

                @pl.when((b <= t) & sent_it & takes_part(t + 1))
                def _():
                    z_copy(0, b, kh, e).wait_send()

                @pl.when((b >= t) & sent_it & takes_part(t - 1))
                def _():
                    z_copy(1, b, kh, e).wait_send()

    for e in range(2):
        def sent(slot):
            for r in range(1, nt):
                dx_copy(r, e, slot).wait_send()
            dx_keep(e, slot).wait()

        each_own(sent)
        for r in range(1, nt):
            for slot in range(slots):
                @pl.when(slot < count((t + nt - r) % nt))
                def _():
                    dx_arrival(r, e, slot).wait_recv()


def copy_kernel(parts, count, *refs):
    sources, targets, held = refs[:count], refs[count:2 * count], refs[2 * count:3 * count]
    in_sem, out_sem = refs[3 * count:]
    inward, outward = [], []
    for i in range(count):
        size = sources[i].shape[-2] // parts
        for k in range(parts):
            index = (0,) * (len(sources[i].shape) - 2) + (pl.ds(k * size, size),)
            inward.append(pltpu.make_async_copy(
                sources[i].at[index], held[i].at[index], in_sem.at[i, k]
            ))
            outward.append(pltpu.make_async_copy(
                held[i].at[index], targets[i].at[index], out_sem.at[i, k]
            ))
    for copy in inward:
        copy.start()
    for arrived, copy in zip(inward, outward):
        arrived.wait()
        copy.start()
    for copy in outward:
        copy.wait()


def to_outputs(arrays):
    hbm = pl.BlockSpec(memory_space=pltpu.HBM)
    parts = 2
    count = len(arrays)
    dma = pltpu.SemaphoreType.DMA
    return pl.pallas_call(
        functools.partial(copy_kernel, parts, count),
        out_shape=tuple(jax.ShapeDtypeStruct(a.shape, a.dtype) for a in arrays),
        in_specs=[hbm] * count,
        out_specs=[hbm] * count,
        scratch_shapes=[pltpu.VMEM(a.shape, a.dtype) for a in arrays]
        + [dma((count, parts)), dma((count, parts))],
    )(*arrays)


def per_device(
    layer_input,
    queries,
    forward_output,
    attention_output_gradient,
    key_weight,
    value_projection_weight,
    segment,
    block_table,
    block_owner,
):
    nt, nd, nc = lax.axis_size("tensor"), lax.axis_size("dp"), lax.axis_size("ctx")
    plane = nd * nc
    half = plane // 2
    rows, width = layer_input.shape[1:]
    query_rows, query_width = queries.shape[1:]
    kv = key_weight.shape[1]
    heads = kv // HEAD_SIZE
    groups = query_width // kv
    blocks = block_owner.shape[1]
    key_rows = nc * query_rows
    end_units, mid_units = UNITS if nt == 4 else (1, 1)
    unit = width // (2 * end_units + (nt - 2) * mid_units)
    slots = max(end_units, mid_units)
    fans = 4 if nt == 4 and nc == 2 and half == 4 and end_units == 0 else half - 1
    slice_width = width // plane
    subs = min(4, rows // 16)
    dma = pltpu.SemaphoreType.DMA
    hbm = pl.BlockSpec(memory_space=pltpu.HBM)
    vmem = pl.BlockSpec(memory_space=pltpu.VMEM)
    smem = pl.BlockSpec(memory_space=pltpu.SMEM)
    query_grad, input_grad, key_weight_grad, value_weight_grad = pl.pallas_call(
        functools.partial(grads_kernel, nt, nd, nc, heads, groups, subs, end_units, mid_units),
        out_shape=(
            jax.ShapeDtypeStruct((1, query_rows, query_width), LOW),
            jax.ShapeDtypeStruct((1, rows, width), LOW),
            jax.ShapeDtypeStruct((slice_width, kv), LOW),
            jax.ShapeDtypeStruct((slice_width, kv), LOW),
        ),
        in_specs=[hbm] * 6 + [vmem, smem, smem],
        out_specs=[vmem] * 4,
        scratch_shapes=[
            pltpu.VMEM((nt * rows, width), LOW),
            pltpu.VMEM((width, 2 * kv), LOW),
            pltpu.VMEM((slots, nt, unit, 2 * kv), LOW),
            pltpu.VMEM((plane, nt, rows, slice_width), LOW),
            pltpu.VMEM((query_rows, query_width), LOW),
            pltpu.VMEM((query_rows, query_width), LOW),
            pltpu.VMEM((query_rows, query_width), LOW),
            pltpu.VMEM((key_rows, 2 * kv), LOW),
            pltpu.VMEM((key_rows, query_rows), FULL),
            pltpu.VMEM((heads * groups, query_rows), FULL),
            pltpu.VMEM((key_rows, 2 * kv), FULL),
            pltpu.VMEM((nc - 1, query_rows, 2 * kv), FULL),
            pltpu.VMEM((nt, 2, query_rows // 2, 2 * kv), LOW),
            pltpu.VMEM((plane * query_rows, 2 * kv), LOW),
            pltpu.VMEM((slots, query_rows, unit), FULL),
            pltpu.VMEM((2, slots, query_rows // 2, unit), LOW),
            dma((2, nt - 1, subs)), dma((2, nt - 1, subs)),
            dma((nt, slots)), dma((nt, slots)),
            dma((nt, plane - 1)), dma((nt, plane - 1)),
            dma((slots, nt, fans)), dma((slots, nt, fans)),
            dma((slots, nt, half)), dma((slots, nt, half)),
            dma((heads, half - 1)), dma((heads, half - 1)),
            dma((heads, half)), dma((heads, half)),
            dma((nc - 1, nt)), dma((nc - 1, nt)),
            dma((heads, nc - 1)), dma((heads, nc - 1)),
            dma((2, nt, heads, 2)), dma((nt, heads, 2)),
            dma((2, slots, nt - 1)), dma((2, slots, nt - 1)),
            dma((4 + 2 * heads,)), dma((3, slots)), dma((nt,)),
        ],
        compiler_params=pltpu.CompilerParams(
            collective_id=0, has_side_effects=True, vmem_limit_bytes=60 << 20
        ),
    )(
        layer_input[0], queries[0], forward_output[0], attention_output_gradient[0],
        key_weight, value_projection_weight,
        segment.reshape(blocks, BLK), block_table[0], block_owner,
    )
    return to_outputs((query_grad, input_grad, key_weight_grad, value_weight_grad))


def solution(mesh):
    in_specs = (
        P("dp", ("ctx", "tensor"), None),
        P("dp", "ctx", "tensor"),
        P("dp", "ctx", "tensor"),
        P("dp", "ctx", "tensor"),
        P(None, "tensor"),
        P(None, "tensor"),
        P("dp", None),
        P("dp", None, None),
        P("dp", None),
    )
    out_specs = (
        P("dp", "ctx", "tensor"),
        P("dp", ("ctx", "tensor"), None),
        P(("dp", "ctx"), "tensor"),
        P(("dp", "ctx"), "tensor"),
    )
    return jax.shard_map(
        per_device, mesh=mesh, in_specs=in_specs, out_specs=out_specs, check_vma=False
    )
```

```python
import functools
import math

import jax
import jax.numpy as jnp
from jax import lax
from jax.experimental import pallas as pl
from jax.experimental.pallas import tpu as pltpu
from jax.sharding import PartitionSpec as P

HEAD_SIZE = 128
BLK = 128
UNITS = (0, 4)

MESH = pl.DeviceIdType.MESH
LOW = jnp.bfloat16
FULL = jnp.float32


def grads_kernel(
    nt, nd, nc, heads, groups, subs, end_units, mid_units,
    x_ref, q_ref, o_ref, do_ref, kw_ref, vw_ref, seg_ref, table_ref, owner_ref,
    qg_ref, dx_ref, dkw_ref, dvw_ref,
    g, kwv, wide, xc, q, o, do, kv, bias, corr, acc, part, kz, kp, dx_sum, dx_send,
    x_send, x_recv, w_send, w_recv, p_send, p_recv, f_send, f_recv, s_send, s_recv,
    m_send, m_recv, n_send, n_recv, k_send, k_recv, c_send, c_recv, z_send, z_recv, d_send, d_recv,
    local_sem, own_sem, keep_sem,
):
    t = lax.axis_index("tensor")
    d = lax.axis_index("dp")
    c = lax.axis_index("ctx")
    plane = nd * nc
    half = plane // 2
    p = d * nc + c
    h = (d // 2) * nc + c
    core = d % 2
    rows, width = x_ref.shape
    kv2 = kwv.shape[1]
    unit = wide.shape[2]
    slots = wide.shape[0]
    piece = unit // plane
    slice_width = width // plane
    query_rows = nt * rows
    key_rows = nc * query_rows
    sub_rows = rows // subs
    hs = HEAD_SIZE
    pair = 2 * hs
    half_rows = rows // 2
    scale = 1.0 / math.sqrt(hs)

    def at(i, size):
        return pl.ds(pl.multiple_of(i * size, size), size)

    def is_end(b):
        return (b == 0) | (b == nt - 1)

    def count(b):
        return jnp.where(is_end(b), end_units, mid_units)

    def first(b):
        return jnp.where(b == 0, 0, end_units + (b - 1) * mid_units)

    def beside_end(b):
        return ring & is_end(b) & ((b == t + 1) | (b == t - 1))

    def takes_part(b):
        return (b >= 0) & (b < nt) & (count(b) > 0)

    far = jnp.where(t < nt // 2, nt - 1, 0)
    ring = nt == 4 and nc == 2 and half == 4 and end_units == 0

    def x_rows(b):
        return g.at[at(b, rows), :]

    def x_copy(way, s, k, first):
        step = 1 if way == 0 else -1
        b = t - step * (s - 1)
        target = t + step
        ok = (target >= 0) & (target < nt) & (b >= 0) & (b < nt)
        dst = g.at[pl.ds(pl.multiple_of(b * rows + k * sub_rows, sub_rows), sub_rows), :]
        src = x_ref.at[pl.ds(k * sub_rows, sub_rows), :] if first else dst
        return ok, pltpu.make_async_remote_copy(
            src_ref=src, dst_ref=dst, send_sem=x_send.at[way, s - 1, k],
            recv_sem=x_recv.at[way, s - 1, k], device_id={"tensor": target}, device_id_type=MESH,
        )

    def w_copy(to, slot, direct):
        share, size = (core, unit // 2) if direct else (p, piece)
        begin = (first(to) + slot) * unit + share * size
        return pltpu.make_async_remote_copy(
            src_ref=kwv.at[pl.ds(pl.multiple_of(begin, size), size), :],
            dst_ref=wide.at[slot, t, at(share, size), :],
            send_sem=w_send.at[to, slot], recv_sem=w_recv.at[t, slot],
            device_id={"tensor": to}, device_id_type=MESH,
        )

    def w_half(b, slot):
        return wide.at[slot, b, at(core, unit // 2), :]

    def w_arrival(b, slot, direct):
        ref = w_half(b, slot) if direct else wide.at[slot, b, at(p, piece), :]
        return pltpu.make_async_remote_copy(
            src_ref=ref, dst_ref=ref, send_sem=w_send.at[b, slot], recv_sem=w_recv.at[b, slot],
            device_id={"tensor": b}, device_id_type=MESH,
        )

    def each_target(direct, action):
        for slot in range(slots):
            for to in range(nt):
                if slot < (end_units if to in (0, nt - 1) else mid_units):
                    beside = is_end(t) & ((t == to + 1) | (t == to - 1)) & ring
                    good = beside if direct else (t != to) & jnp.logical_not(beside)

                    @pl.when(good)
                    def _():
                        action(w_copy(to, slot, direct), to)

    def send_weights(direct, condition):
        def send(copy, to):
            @pl.when(condition(to))
            def _():
                copy.start()

        each_target(direct, send)

    def plane_copy(b, r, source):
        other = (p + r) % plane
        return pltpu.make_async_remote_copy(
            src_ref=source.at[:, at(other, slice_width)], dst_ref=xc.at[p, b],
            send_sem=p_send.at[b, r - 1], recv_sem=p_recv.at[b, r - 1],
            device_id={"dp": other // nc, "ctx": other % nc}, device_id_type=MESH,
        )

    def to_plane(b, source):
        for r in range(1, plane):
            plane_copy(b, r, source).start()

    def keep_copy(b):
        return pltpu.make_async_copy(
            x_rows(b).at[:, at(p, slice_width)], xc.at[p, b], keep_sem.at[b]
        )

    def kv_copy(j, b):
        own = kv.at[pl.ds(pl.multiple_of(c * query_rows + b * rows, rows), rows), :]
        return pltpu.make_async_remote_copy(
            src_ref=own, dst_ref=own, send_sem=k_send.at[j - 1, b], recv_sem=k_recv.at[j - 1, b],
            device_id={"ctx": (c + j) % nc}, device_id_type=MESH,
        )

    def same_core(j):
        hh = (h + half - j) % half
        return {"dp": (hh // nc) * 2 + core, "ctx": hh % nc}, (
            ((hh // nc) * 2 + core) * nc + hh % nc
        )

    sibling = {"dp": d + 1 - 2 * core}

    def wide_at(slot, b, other, lo=0, size=None):
        return wide.at[
            slot, b, pl.ds(pl.multiple_of(other * piece + lo, 16), size or piece), :
        ]

    beside_x = d * nc + (c + 1) % nc
    beside_y = ((d + 2) % nd) * nc + c
    across = ((d + 2) % nd) * nc + (c + 1) % nc

    def fan_copy(b, slot, j):
        if ring:
            lower = piece // 2
            ref, to = (
                (wide_at(slot, b, p), {"ctx": (c + 1) % nc}),
                (wide_at(slot, b, p), {"dp": (d + 2) % nd}),
                (wide_at(slot, b, beside_x, 0, lower), {"dp": (d + 2) % nd}),
                (wide_at(slot, b, beside_y, lower, lower), {"ctx": (c + 1) % nc}),
            )[j]
        else:
            ref, to = wide_at(slot, b, p), same_core(half - 1 - j)[0]
        return pltpu.make_async_remote_copy(
            src_ref=ref, dst_ref=ref, send_sem=f_send.at[slot, b, j],
            recv_sem=f_recv.at[slot, b, j], device_id=to, device_id_type=MESH,
        )

    def sibling_copy(b, slot, j):
        if ring:
            other = (p, beside_x, beside_y, across)[j]
        else:
            other = same_core(j)[1]
        ref = wide_at(slot, b, other)
        return pltpu.make_async_remote_copy(
            src_ref=ref, dst_ref=ref, send_sem=s_send.at[slot, b, j],
            recv_sem=s_recv.at[slot, b, j], device_id=sibling, device_id_type=MESH,
        )

    fans = 4 if ring else half - 1

    def each_weight(condition, action):
        for b in range(nt):
            for slot in range(slots):
                @pl.when((b != t) & (slot < count(t)) & condition(b))
                def _():
                    action(b, slot)

    def half_copy(b, slot):
        ref = w_half(b, slot)
        return pltpu.make_async_remote_copy(
            src_ref=ref, dst_ref=ref, send_sem=s_send.at[slot, b, 0],
            recv_sem=s_recv.at[slot, b, 0], device_id=sibling, device_id_type=MESH,
        )

    def pass_half(b, slot):
        w_arrival(b, slot, True).wait_recv()
        half_copy(b, slot).start()

    def spread_first(b, slot):
        w_arrival(b, slot, False).wait_recv()
        for j in range(2 if ring else fans):
            fan_copy(b, slot, j).start()
        sibling_copy(b, slot, 0).start()

    def spread_second(b, slot):
        if ring:
            for j in range(2):
                fan_copy(b, slot, j).wait_recv()
                fan_copy(b, slot, 2 + j).start()
                sibling_copy(b, slot, 1 + j).start()

    def spread_third(b, slot):
        if ring:
            for j in (2, 3):
                fan_copy(b, slot, j).wait_recv()
            sibling_copy(b, slot, 3).start()
        else:
            for j in range(fans):
                fan_copy(b, slot, j).wait_recv()
                sibling_copy(b, slot, j + 1).start()

    def early(b):
        return beside_end(b)

    def late(b):
        return jnp.logical_not(beside_end(b))

    def inner_late(b):
        return late(b) & jnp.logical_not(is_end(b))

    def outer_late(b):
        return late(b) & is_end(b)

    def cols(kh):
        return pl.ds(kh * pair, pair)

    def part_copy(j, kh):
        other = (c + j) % nc
        return pltpu.make_async_remote_copy(
            src_ref=acc.at[at(other, query_rows), cols(kh)], dst_ref=part.at[j - 1, :, cols(kh)],
            send_sem=c_send.at[kh, j - 1], recv_sem=c_recv.at[kh, j - 1],
            device_id={"ctx": other}, device_id_type=MESH,
        )

    def z_copy(way, b, kh, e):
        ref = kz.at[b, e, :, cols(kh)]
        return pltpu.make_async_remote_copy(
            src_ref=ref, dst_ref=ref, send_sem=z_send.at[way, b, kh, e],
            recv_sem=z_recv.at[b, kh, e], device_id={"tensor": t + 1 - 2 * way},
            device_id_type=MESH,
        )

    def kp_at(other, kh):
        return kp.at[at(other, query_rows), cols(kh)]

    def kp_copy(j, kh):
        return pltpu.make_async_remote_copy(
            src_ref=kp_at(p, kh), dst_ref=kp_at(p, kh), send_sem=m_send.at[kh, j],
            recv_sem=m_recv.at[kh, j], device_id=same_core(half - 1 - j)[0],
            device_id_type=MESH,
        )

    def kp_sibling(j, kh):
        ref = kp_at(same_core(j)[1], kh)
        return pltpu.make_async_remote_copy(
            src_ref=ref, dst_ref=ref, send_sem=n_send.at[kh, j], recv_sem=n_recv.at[kh, j],
            device_id=sibling, device_id_type=MESH,
        )

    def dx_columns(b, slot):
        return pl.ds(pl.multiple_of((first(b) + slot) * unit, unit), unit)

    def dx_copy(r, e, slot):
        other = (t + r) % nt
        return pltpu.make_async_remote_copy(
            src_ref=dx_send.at[e, slot, at(other, half_rows), :],
            dst_ref=dx_ref.at[0, pl.ds(e * half_rows, half_rows), dx_columns(t, slot)],
            send_sem=d_send.at[e, slot, r - 1], recv_sem=d_recv.at[e, slot, r - 1],
            device_id={"tensor": other}, device_id_type=MESH,
        )

    def dx_arrival(r, e, slot):
        b = (t + nt - r) % nt
        ref = dx_ref.at[0, pl.ds(e * half_rows, half_rows), dx_columns(b, slot)]
        return pltpu.make_async_remote_copy(
            src_ref=ref, dst_ref=ref, send_sem=d_send.at[e, slot, r - 1],
            recv_sem=d_recv.at[e, slot, r - 1], device_id={"tensor": b}, device_id_type=MESH,
        )

    def dx_keep(e, slot):
        return pltpu.make_async_copy(
            dx_send.at[e, slot, at(t, half_rows), :],
            dx_ref.at[0, pl.ds(e * half_rows, half_rows), dx_columns(t, slot)],
            own_sem.at[1 + e, slot],
        )

    loads = [
        pltpu.make_async_copy(x_ref, x_rows(t), local_sem.at[0]),
        pltpu.make_async_copy(q_ref, q, local_sem.at[1]),
        pltpu.make_async_copy(o_ref, o, local_sem.at[2]),
        pltpu.make_async_copy(do_ref, do, local_sem.at[3]),
    ]
    weight_loads = []
    for kh in range(heads):
        for which, ref in enumerate((kw_ref, vw_ref)):
            weight_loads.append(pltpu.make_async_copy(
                ref.at[:, pl.ds(kh * hs, hs)], kwv.at[:, pl.ds(kh * pair + which * hs, hs)],
                local_sem.at[4 + 2 * kh + which],
            ))
    for copy in loads + weight_loads:
        copy.start()
    barrier = pltpu.get_barrier_semaphore()
    for r in range(1, nt):
        pl.semaphore_signal(
            barrier, inc=1, device_id={"tensor": (t + r) % nt}, device_id_type=MESH
        )
    for r in range(1, plane):
        other = (p + r) % plane
        pl.semaphore_signal(
            barrier, inc=1, device_id={"dp": other // nc, "ctx": other % nc}, device_id_type=MESH
        )
    pl.semaphore_wait(barrier, nt - 1 + plane - 1)

    for k in range(subs):
        for way in (0, 1):
            ok, copy = x_copy(way, 1, k, True)

            @pl.when(ok)
            def _():
                copy.start()

    to_plane(t, x_ref)
    for copy in loads + weight_loads:
        copy.wait()
    keep_copy(t).start()
    def own_wide(slot):
        return pltpu.make_async_copy(
            kwv.at[pl.ds(pl.multiple_of((first(t) + slot) * unit, unit), unit), :],
            wide.at[slot, t], own_sem.at[0, slot],
        )

    def each_own(action):
        for slot in range(slots):
            @pl.when(slot < count(t))
            def _():
                action(slot)

    each_own(lambda slot: own_wide(slot).start())
    send_weights(True, lambda to: True)

    def iota(axis):
        return lax.broadcasted_iota(jnp.int32, (BLK, BLK), axis)

    blocks = key_rows // BLK
    blocks_here = query_rows // BLK

    @pl.loop(0, blocks)
    def _(kb):
        key_owner = owner_ref[0, kb]
        key_seg = jnp.sum(
            jnp.where(iota(0) == iota(1), seg_ref[pl.ds(key_owner, 1), :], 0), axis=1,
            keepdims=True,
        )
        for qb in range(blocks_here):
            query_owner = owner_ref[0, c * blocks_here + qb]
            query_seg = seg_ref[pl.ds(query_owner, 1), :]
            withheld = 1 - table_ref[query_owner, key_owner]
            key_pos = iota(0) + (key_owner * BLK + withheld * (1 << 20))
            query_pos = iota(1) + query_owner * BLK
            same = (key_seg == 0) | (key_seg == query_seg)
            bias[at(kb, BLK), pl.ds(qb * BLK, BLK)] = jnp.where(
                (key_pos <= query_pos) & same, 0.0, -jnp.inf
            )

    @pl.loop(0, heads * groups)
    def _(i):
        head = at(i, hs)
        product = do[:, head].astype(FULL) * o[:, head].astype(FULL)
        corr[pl.ds(i, 1), :] = jnp.sum(product.T, axis=0, keepdims=True)

    depth = min(1024, width)

    def project(b):
        def step(i, total):
            return total + jnp.dot(
                g[at(b, rows), at(i, depth)], kwv[at(i, depth), :], preferred_element_type=FULL
            )

        total = lax.fori_loop(0, width // depth, step, jnp.zeros((rows, kv2), FULL))
        kv[pl.ds(pl.multiple_of(c * query_rows + b * rows, rows), rows), :] = total.astype(LOW)
        for j in range(1, nc):
            kv_copy(j, b).start()

    project(t)
    for s in range(1, nt):
        for k in range(subs):
            for way in (0, 1):
                b = t - s if way == 0 else t + s

                @pl.when((b >= 0) & (b < nt))
                def _():
                    x_copy(way, s, k, False)[1].wait_recv()

                if s < nt - 1:
                    ok, copy = x_copy(way, s + 1, k, False)

                    @pl.when(ok)
                    def _():
                        copy.start()

        for way in (0, 1):
            b = t - s if way == 0 else t + s

            @pl.when((b >= 0) & (b < nt))
            def _():
                project(b)
                keep_copy(b).start()

            @pl.when((b >= 0) & (b < nt) & (b != far))
            def _():
                to_plane(b, x_rows(b))

        if s == 1:
            send_weights(False, lambda to: (not to in (0, nt - 1)) & jnp.logical_not(is_end(t)))
            send_weights(False, lambda to: (not to in (0, nt - 1)) & is_end(t))
        if s == nt // 2:
            each_weight(inner_late, spread_first)

    send_weights(False, lambda to: is_end(t) & (to in (0, nt - 1)))
    for j in range(1, nc):
        for b in range(nt):
            kv_copy(j, b).wait_recv()

    acc[...] = jnp.zeros_like(acc)
    stack = math.gcd(groups, max(1, 2048 // key_rows))
    for kh in range(heads):
        key_cols = pl.ds(kh * pair, hs)
        value_cols = pl.ds(kh * pair + hs, hs)

        @pl.loop(0, groups // stack)
        def _(i):
            picked = [kh * groups + i * stack + n for n in range(stack)]
            lanes = [pl.ds(pl.multiple_of(head * hs, hs), hs) for head in picked]
            keys = kv[:, key_cols]
            queries = jnp.concatenate([q[:, head] for head in lanes], axis=0)
            grads = jnp.concatenate([do[:, head] for head in lanes], axis=0)
            scores = lax.dot_general(
                keys, queries, (((1,), (1,)), ((), ())), preferred_element_type=FULL
            )
            scores = scores * (scale * math.log2(math.e)) + jnp.concatenate(
                [bias[...]] * stack, axis=1
            )
            top = jnp.max(scores, axis=0, keepdims=True)
            weights = jnp.exp2(scores - top)
            probs = weights * (1.0 / jnp.sum(weights, axis=0, keepdims=True))
            acc[:, value_cols] += jnp.dot(
                probs.astype(LOW), grads, preferred_element_type=FULL
            )
            prob_grads = lax.dot_general(
                kv[:, value_cols], grads, (((1,), (1,)), ((), ())), preferred_element_type=FULL
            )
            corrections = jnp.concatenate([corr[pl.ds(head, 1), :] for head in picked], axis=1)
            score_grads = (probs * (prob_grads - corrections)).astype(LOW)
            acc[:, key_cols] += jnp.dot(score_grads, queries, preferred_element_type=FULL)
            query_grads = lax.dot_general(
                score_grads, keys, (((0,), (0,)), ((), ())), preferred_element_type=FULL
            )
            for n, head in enumerate(lanes):
                rows_n = slice(n * query_rows, (n + 1) * query_rows)
                qg_ref[0, :, head] = (query_grads[rows_n] * scale).astype(LOW)

        acc[:, key_cols] = acc[:, key_cols] * scale
        for j in range(1, nc):
            part_copy(j, kh).start()
        if kh == 0:
            each_weight(inner_late, spread_second)
            each_weight(outer_late, spread_first)

    send_weights(False, lambda to: jnp.logical_not(is_end(t)) & (to in (0, nt - 1)))

    each_weight(inner_late, spread_third)
    each_weight(outer_late, spread_second)

    for kh in range(heads):
        for j in range(1, nc):
            part_copy(j, kh).wait_recv()
        total = acc[at(c, query_rows), cols(kh)]
        for j in range(1, nc):
            total = total + part[j - 1, :, cols(kh)]
        total = total.astype(LOW)
        kp[at(p, query_rows), cols(kh)] = total
        by_half = total.reshape(nt, 2, half_rows, pair)
        for e in range(2):
            kz[t, e, :, cols(kh)] = by_half[:, e].reshape(nt * half_rows, pair)
            for way in (0, 1):
                @pl.when(takes_part(t + 1 - 2 * way))
                def _():
                    z_copy(way, t, kh, e).start()

    each_weight(early, pass_half)
    for kh in range(heads):
        for j in range(half - 1):
            kp_copy(j, kh).start()
        kp_sibling(0, kh).start()
    ends = (0, nt - 1)
    inner = [b for b in range(nt) if b not in ends]
    near = jnp.where(t < nt // 2, 0, nt - 1)
    tile = min(256, unit)

    def relay(b, kh, e):
        @pl.when((b != t) & takes_part(t))
        def _():
            z_copy(0, b, kh, e).wait_recv()

        @pl.when((b < t) & takes_part(t) & takes_part(t + 1))
        def _():
            z_copy(0, b, kh, e).start()

        @pl.when((b > t) & takes_part(t) & takes_part(t - 1))
        def _():
            z_copy(1, b, kh, e).start()

    def product(left, slot, b, columns):
        return lax.dot_general(
            left, wide[slot, b, columns, :], (((1,), (1,)), ((), ())),
            preferred_element_type=FULL,
        )

    for b in sorted(inner, key=lambda b: abs(2 * b - nt + 1)):
        for kh in range(heads):
            for e in range(2):
                relay(b, kh, e)
    each_own(lambda slot: own_wide(slot).wait())

    def spread_done(b, slot):
        for j in range(half):
            sibling_copy(b, slot, j).wait_recv()

    def input_grads_inner(slot):
        @pl.loop(0, unit // tile)
        def _(n):
            columns = at(n, tile)
            out = None
            for b in inner:
                term = product(kz[b].reshape(query_rows, kv2), slot, b, columns)
                out = term if out is None else out + term
            dx_sum[slot, :, columns] = out

    each_weight(inner_late, spread_done)
    each_own(input_grads_inner)
    for kh in range(heads):
        for e in range(2):
            relay(near, kh, e)
    each_weight(early, lambda b, slot: half_copy(b, slot).wait_recv())
    if ring:
        each_weight(outer_late, spread_third)
        each_weight(outer_late, spread_done)
    else:
        each_weight(outer_late, spread_third)
        each_weight(outer_late, spread_done)
    to_plane(far, x_rows(far))

    for e in range(2):
        for kh in range(heads):
            relay(far, kh, e)

        def input_grads(slot):
            @pl.loop(0, unit // tile)
            def _(n):
                columns = at(n, tile)
                part_rows = pl.ds(e * nt * half_rows, nt * half_rows)
                dx_send[e, slot, :, columns] = (
                    dx_sum[slot, part_rows, columns] + product(kz[near, e], slot, near, columns)
                    + product(kz[far, e], slot, far, columns)
                ).astype(LOW)

            for r in sorted(range(1, nt), key=lambda r: abs(2 * r - nt)):
                dx_copy(r, e, slot).start()
            dx_keep(e, slot).start()

        each_own(input_grads)

    for b in range(nt):
        for r in range(1, plane):
            plane_copy(b, r, x_ref).wait_recv()
        keep_copy(b).wait()
    for kh in range(heads):
        for j in range(half - 1):
            kp_copy(j, kh).wait_recv()
            kp_sibling(j + 1, kh).start()
    for kh in range(heads):
        for j in range(half):
            kp_sibling(j, kh).wait_recv()
    step_width = min(256, slice_width)
    plane_rows = xc.reshape(plane * nt * rows, slice_width)

    @pl.loop(0, slice_width // step_width)
    def _(m):
        columns = at(m, step_width)
        out = lax.dot_general(
            plane_rows[:, columns], kp[...], (((0,), (0,)), ((), ())),
            preferred_element_type=FULL,
        ).astype(LOW)
        for kh in range(heads):
            dkw_ref[columns, pl.ds(kh * hs, hs)] = out[:, kh * pair:kh * pair + hs]
            dvw_ref[columns, pl.ds(kh * hs, hs)] = out[:, kh * pair + hs:(kh + 1) * pair]

    for s in range(1, nt):
        for k in range(subs):
            for way in (0, 1):
                ok, copy = x_copy(way, s, k, s == 1)

                @pl.when(ok)
                def _():
                    copy.wait_send()

    for direct in (False, True):
        each_target(direct, lambda copy, to: copy.wait_send())

    def spread_sent(b, slot):
        for j in range(fans):
            fan_copy(b, slot, j).wait_send()
        for j in range(half):
            sibling_copy(b, slot, j).wait_send()

    each_weight(late, spread_sent)
    each_weight(early, lambda b, slot: half_copy(b, slot).wait_send())
    for b in range(nt):
        for r in range(1, plane):
            plane_copy(b, r, x_ref).wait_send()
        for j in range(1, nc):
            kv_copy(j, b).wait_send()
    for kh in range(heads):
        for j in range(1, nc):
            part_copy(j, kh).wait_send()
        for j in range(half - 1):
            kp_copy(j, kh).wait_send()
        for j in range(half):
            kp_sibling(j, kh).wait_send()
        for e in range(2):
            for b in range(nt):
                sent_it = (b == t) | takes_part(t)

                @pl.when((b <= t) & sent_it & takes_part(t + 1))
                def _():
                    z_copy(0, b, kh, e).wait_send()

                @pl.when((b >= t) & sent_it & takes_part(t - 1))
                def _():
                    z_copy(1, b, kh, e).wait_send()

    for e in range(2):
        def sent(slot):
            for r in range(1, nt):
                dx_copy(r, e, slot).wait_send()
            dx_keep(e, slot).wait()

        each_own(sent)
        for r in range(1, nt):
            for slot in range(slots):
                @pl.when(slot < count((t + nt - r) % nt))
                def _():
                    dx_arrival(r, e, slot).wait_recv()


def copy_kernel(parts, count, *refs):
    sources, targets, held = refs[:count], refs[count:2 * count], refs[2 * count:3 * count]
    in_sem, out_sem = refs[3 * count:]
    inward, outward = [], []
    for i in range(count):
        size = sources[i].shape[-2] // parts
        for k in range(parts):
            index = (0,) * (len(sources[i].shape) - 2) + (pl.ds(k * size, size),)
            inward.append(pltpu.make_async_copy(
                sources[i].at[index], held[i].at[index], in_sem.at[i, k]
            ))
            outward.append(pltpu.make_async_copy(
                held[i].at[index], targets[i].at[index], out_sem.at[i, k]
            ))
    for copy in inward:
        copy.start()
    for arrived, copy in zip(inward, outward):
        arrived.wait()
        copy.start()
    for copy in outward:
        copy.wait()


def to_outputs(arrays):
    hbm = pl.BlockSpec(memory_space=pltpu.HBM)
    parts = 4
    count = len(arrays)
    dma = pltpu.SemaphoreType.DMA
    return pl.pallas_call(
        functools.partial(copy_kernel, parts, count),
        out_shape=tuple(jax.ShapeDtypeStruct(a.shape, a.dtype) for a in arrays),
        in_specs=[hbm] * count,
        out_specs=[hbm] * count,
        scratch_shapes=[pltpu.VMEM(a.shape, a.dtype) for a in arrays]
        + [dma((count, parts)), dma((count, parts))],
    )(*arrays)


def per_device(
    layer_input,
    queries,
    forward_output,
    attention_output_gradient,
    key_weight,
    value_projection_weight,
    segment,
    block_table,
    block_owner,
):
    nt, nd, nc = lax.axis_size("tensor"), lax.axis_size("dp"), lax.axis_size("ctx")
    plane = nd * nc
    half = plane // 2
    rows, width = layer_input.shape[1:]
    query_rows, query_width = queries.shape[1:]
    kv = key_weight.shape[1]
    heads = kv // HEAD_SIZE
    groups = query_width // kv
    blocks = block_owner.shape[1]
    key_rows = nc * query_rows
    end_units, mid_units = UNITS if nt == 4 else (1, 1)
    unit = width // (2 * end_units + (nt - 2) * mid_units)
    slots = max(end_units, mid_units)
    fans = 4 if nt == 4 and nc == 2 and half == 4 and end_units == 0 else half - 1
    slice_width = width // plane
    subs = min(4, rows // 16)
    dma = pltpu.SemaphoreType.DMA
    hbm = pl.BlockSpec(memory_space=pltpu.HBM)
    vmem = pl.BlockSpec(memory_space=pltpu.VMEM)
    smem = pl.BlockSpec(memory_space=pltpu.SMEM)
    query_grad, input_grad, key_weight_grad, value_weight_grad = pl.pallas_call(
        functools.partial(grads_kernel, nt, nd, nc, heads, groups, subs, end_units, mid_units),
        out_shape=(
            jax.ShapeDtypeStruct((1, query_rows, query_width), LOW),
            jax.ShapeDtypeStruct((1, rows, width), LOW),
            jax.ShapeDtypeStruct((slice_width, kv), LOW),
            jax.ShapeDtypeStruct((slice_width, kv), LOW),
        ),
        in_specs=[hbm] * 6 + [vmem, smem, smem],
        out_specs=[vmem] * 4,
        scratch_shapes=[
            pltpu.VMEM((nt * rows, width), LOW),
            pltpu.VMEM((width, 2 * kv), LOW),
            pltpu.VMEM((slots, nt, unit, 2 * kv), LOW),
            pltpu.VMEM((plane, nt, rows, slice_width), LOW),
            pltpu.VMEM((query_rows, query_width), LOW),
            pltpu.VMEM((query_rows, query_width), LOW),
            pltpu.VMEM((query_rows, query_width), LOW),
            pltpu.VMEM((key_rows, 2 * kv), LOW),
            pltpu.VMEM((key_rows, query_rows), FULL),
            pltpu.VMEM((heads * groups, query_rows), FULL),
            pltpu.VMEM((key_rows, 2 * kv), FULL),
            pltpu.VMEM((nc - 1, query_rows, 2 * kv), FULL),
            pltpu.VMEM((nt, 2, query_rows // 2, 2 * kv), LOW),
            pltpu.VMEM((plane * query_rows, 2 * kv), LOW),
            pltpu.VMEM((slots, query_rows, unit), FULL),
            pltpu.VMEM((2, slots, query_rows // 2, unit), LOW),
            dma((2, nt - 1, subs)), dma((2, nt - 1, subs)),
            dma((nt, slots)), dma((nt, slots)),
            dma((nt, plane - 1)), dma((nt, plane - 1)),
            dma((slots, nt, fans)), dma((slots, nt, fans)),
            dma((slots, nt, half)), dma((slots, nt, half)),
            dma((heads, half - 1)), dma((heads, half - 1)),
            dma((heads, half)), dma((heads, half)),
            dma((nc - 1, nt)), dma((nc - 1, nt)),
            dma((heads, nc - 1)), dma((heads, nc - 1)),
            dma((2, nt, heads, 2)), dma((nt, heads, 2)),
            dma((2, slots, nt - 1)), dma((2, slots, nt - 1)),
            dma((4 + 2 * heads,)), dma((3, slots)), dma((nt,)),
        ],
        compiler_params=pltpu.CompilerParams(
            collective_id=0, has_side_effects=True, vmem_limit_bytes=60 << 20
        ),
    )(
        layer_input[0], queries[0], forward_output[0], attention_output_gradient[0],
        key_weight, value_projection_weight,
        segment.reshape(blocks, BLK), block_table[0], block_owner,
    )
    return to_outputs((query_grad, input_grad, key_weight_grad, value_weight_grad))


def solution(mesh):
    in_specs = (
        P("dp", ("ctx", "tensor"), None),
        P("dp", "ctx", "tensor"),
        P("dp", "ctx", "tensor"),
        P("dp", "ctx", "tensor"),
        P(None, "tensor"),
        P(None, "tensor"),
        P("dp", None),
        P("dp", None, None),
        P("dp", None),
    )
    out_specs = (
        P("dp", "ctx", "tensor"),
        P("dp", ("ctx", "tensor"), None),
        P(("dp", "ctx"), "tensor"),
        P(("dp", "ctx"), "tensor"),
    )
    return jax.shard_map(
        per_device, mesh=mesh, in_specs=in_specs, out_specs=out_specs, check_vma=False
    )
```
